512 devices in a mesh: row: 32 (over z_hi, y, core), col: 16 (over z_lo, x).
Axes of the slice: x: 4, y: 4, z: 16 (z_hi: 4, z_lo: 4; z = z_hi * 4 + z_lo), core: 2. Of those that a mesh axis runs over, the one named last changes fastest.
Arguments:
- hidden: bfloat16 [256, 2048], P('row', 'col'), may hold values from -60 to 60
- queries: bfloat16 [256, 4096], P('row'), may hold values from -6 to 6
- new_kv: bfloat16 [256, 2, 2048], P('row'), may hold values from -12 to 12
- prompt_kv: bfloat16 [32, 2, 1024, 2048], P('row', None, 'col'), may hold values from -180 to 180
- suffix_kv: bfloat16 [256, 2, 128, 2048], P('row', None, 'col'), may hold values from -12 to 12
- lengths: int32 [256], P('row'), may hold values from 1 to 128, as said below
- w_out: bfloat16 [4096, 2048], P(None, 'col'), may hold values from -0.375 to 0.375
- moe_gain: bfloat16 [2048], P('col'), may hold values from 0.099609375 to 1.8984375
- w_router: bfloat16 [2048, 8], P('col'), may hold values from -0.5 to 0.5
- expert_weights: bfloat16 [8, 5632, 3, 2048], P(None, 'row', None, 'col'), may hold values from -0.25 to 0.25
- old_lines: int32 [8, 5632], replicated, may hold values from 0 to 5631, as said below
- new_lines: int32 [8, 5632], replicated, may hold values from 0 to 5631, as said below
- routes: int32 [256, 2], replicated, may hold values from 0 to 7, all different within a row
Outputs:
- layer_out: float32 [256, 2048], P('row', 'col')
- moved_weights: bfloat16 [8, 5632, 3, 2048], P(None, 'row', None, 'col')
The draws below stay inside these ranges and needn't reach their ends.
Inputs may be any that keep to these rules, and one draw needn't show every extreme that they name: `lengths`: some sequence has all 128 slots filled. `old_lines`: each row is a permutation of the hidden units of one expert; stored lines [j * 176, (j + 1) * 176) lie on row index j. `new_lines`: each row is a permutation of the hidden units of one expert. Counting all experts together, exactly 44 of the lines that one row index holds under old_lines are held by each row index under new_lines. `routes`: the two experts of a token differ.
All inputs are finite; a program needn't handle non-finite values.
Results may differ from the reference program's by a relative error of at most 0.04.
Values may be sent and summed in bfloat16 or wider, within the bound.
A program may use at most 64 MiB of HBM per device.

```python
import jax
import jax.numpy as jnp
from jax import lax

D = 2048
HEADS = 32
KVH = 16
HD = 128
E = 8
FF = 5632
TOPK = 2
SEQ_G = 8
PROMPT = 1024
SUF = 128
G = 32
REP = 2
TOKENS = 256


def draw_hidden(key, part):
    key_values = jax.random.fold_in(key, 0)
    feature_ramp = 1.0 + 2.0 * jnp.arange(D, dtype=jnp.float32) / (D - 1)
    values_base = 0.3 * jnp.clip(jax.random.normal(key_values, (TOKENS, D), jnp.float32), -6.0, 6.0)
    return (values_base * feature_ramp[None, :]).astype(jnp.bfloat16)


def draw_prompt_kv(key, part):
    key_values = jax.random.fold_in(key, 0)
    shape_all = (G, 2, PROMPT, KVH * HD)
    return (2.0 * jnp.clip(jax.random.normal(key_values, shape_all, jnp.float32), -6.0, 6.0)).astype(jnp.bfloat16)


def draw_lengths(key, part):
    key_values, key_spot = jax.random.split(key)
    filled = jax.random.randint(key_values, (TOKENS,), 1, SUF + 1)
    spot_index = jax.random.randint(key_spot, (), 0, TOKENS)
    return jnp.where(jnp.arange(TOKENS) == spot_index, SUF, filled).astype(jnp.int32)


def line_tables(key):
    base_key = jax.random.fold_in(key, 4242)
    key_old, key_shuffle, key_order = jax.random.split(base_key, 3)
    line_count = FF // G
    old_table = jax.vmap(lambda item_key: jax.random.permutation(item_key, FF))(jax.random.split(key_old, E)).astype(jnp.int32)
    source_ids = jnp.arange(G, dtype=jnp.int32)[:, None, None]
    target_ids = jnp.arange(G, dtype=jnp.int32)[None, :, None]
    expert_ids = jnp.arange(E, dtype=jnp.int32)[None, None, :]
    extra_one = jnp.where(line_count % G > 0, ((source_ids + target_ids + expert_ids) % 2 == 0).astype(jnp.int32), 0)
    counts = line_count // G + extra_one
    bounds = jnp.transpose(jnp.cumsum(counts, axis=1), (0, 2, 1))
    slot_ids = jnp.arange(line_count, dtype=jnp.int32)
    target = jnp.sum((bounds[:, :, None, :] <= slot_ids[None, None, :, None]).astype(jnp.int32), axis=-1)
    shuffles = jax.vmap(lambda item_key: jax.random.permutation(item_key, line_count))(jax.random.split(key_shuffle, G * E))
    shuffles = shuffles.reshape(G, E, line_count).astype(jnp.int32)
    stored = source_ids * line_count + shuffles
    stored_by_expert = jnp.transpose(stored, (1, 0, 2)).reshape(E, FF)
    target_by_expert = jnp.transpose(target, (1, 0, 2)).reshape(E, FF)
    tie_break = jax.vmap(lambda item_key: jax.random.permutation(item_key, FF))(jax.random.split(key_order, E)).astype(jnp.int32)
    sort_order = jnp.argsort(target_by_expert * FF + tie_break, axis=1)
    chosen = jnp.take_along_axis(stored_by_expert, sort_order, axis=1)
    new_table = jnp.take_along_axis(old_table, chosen, axis=1)
    return (old_table.astype(jnp.int32), new_table.astype(jnp.int32))


def draw_old_lines(key, part):
    return line_tables(key)[0]


def draw_new_lines(key, part):
    return line_tables(key)[1]


def level_of(own_key, shape, shards, low, top_value):
    gain, own = 1.0, jax.random.fold_in(own_key, 6)
    for axis_at, blocks in shards:
        heights = jnp.exp(jax.random.uniform(jax.random.fold_in(own, axis_at), (blocks,), jnp.float32, low / len(shards), top_value / len(shards)))
        gain = gain * jnp.repeat(heights, shape[axis_at] // blocks).reshape([-1 if axis == axis_at else 1 for axis in range(len(shape))])
    return gain


def different_ones(own_key, rows, amount, top, lift):
    sequence = jax.random.permutation(jax.random.fold_in(own_key, 1), amount)
    favour = sequence
    for power in range(3):
        favour = favour * favour // amount
    favour = favour * lift // amount
    tickets = jax.random.randint(jax.random.fold_in(own_key, 2), (rows, amount), 0, 4096) + favour
    sure = jax.random.permutation(jax.random.fold_in(own_key, 3), rows)[jnp.arange(amount) % rows]
    tickets = jnp.where(jnp.arange(rows)[:, None] == sure[None, :], 1 << 14, tickets)
    priority = tickets * amount + jnp.arange(amount)
    return lax.top_k(priority.astype(jnp.int32), top)[1].astype(jnp.int32)


def scatter_about(rng, shape, scale, bound, cuts=(), held_as=jnp.bfloat16):
    gain = level_of(rng, shape, cuts, -0.22, 0.18) if cuts else 1.0
    array = jax.random.normal(rng, shape, jnp.float32) * scale * gain
    return jnp.minimum(jnp.maximum(array, -bound), bound).astype(held_as)


def setup_inputs(seed: int = 0) -> dict:
    splits = jax.random.split(jax.random.key(seed), 14)
    hidden = draw_hidden(jax.random.fold_in(splits[13], 71), 0)
    queries = scatter_about(splits[1], (TOKENS, HEADS * HD), 1.0, 6.0, ((0, 32),))
    new_kv = scatter_about(splits[2], (TOKENS, 2, KVH * HD), 2.0, 12.0, ((0, 32),))
    prompt_kv = draw_prompt_kv(jax.random.fold_in(splits[13], 71), 0)
    suffix_kv = scatter_about(splits[4], (TOKENS, 2, SUF, KVH * HD), 2.0, 12.0, ((0, 32), (2, 16)))
    lengths = draw_lengths(jax.random.fold_in(splits[13], 71), 0)
    w_out = scatter_about(splits[6], (HEADS * HD, D), (HEADS * HD // 16) ** -0.5, 0.375, ((1, 16),))
    moe_gain = jnp.clip(1.0 + 0.18 * jax.random.normal(splits[7], (D,), jnp.float32), 0.099609375, 1.8984375).astype(jnp.bfloat16)
    w_router = scatter_about(splits[8], (D, E), (D // 16) ** -0.5, 0.5, ((0, 16),))
    expert_weights = scatter_about(splits[9], (E, FF, 3, D), (D // 4) ** -0.5, 0.25, ((1, 32), (3, 16)))
    old_lines = draw_old_lines(jax.random.fold_in(splits[13], 71), 0)
    new_lines = draw_new_lines(jax.random.fold_in(splits[13], 71), 0)
    routes = different_ones(splits[12], TOKENS, E, TOPK, 4096)
    return {"hidden": hidden, "queries": queries, "new_kv": new_kv, "prompt_kv": prompt_kv, "suffix_kv": suffix_kv, "lengths": lengths, "w_out": w_out, "moe_gain": moe_gain, "w_router": w_router, "expert_weights": expert_weights, "old_lines": old_lines, "new_lines": new_lines, "routes": routes}


norm_eps = 1e-06
neg_big = -1e+30

def round_trip(values):
    return lax.optimization_barrier(values.astype(jnp.bfloat16)).astype(jnp.float32)

def group_attention(queries, new_kv, prompt_kv, suffix_kv, lengths, group_index):
    first_row = (group_index * SEQ_G).astype(jnp.int32)
    query_rows = lax.dynamic_slice_in_dim(queries, first_row, SEQ_G, 0).astype(jnp.float32)
    query_heads = query_rows.reshape(SEQ_G, KVH, REP, HD)
    own_pairs = lax.dynamic_slice_in_dim(new_kv, first_row, SEQ_G, 0).astype(jnp.float32)
    own_keys = own_pairs[:, 0].reshape(SEQ_G, KVH, HD)
    own_values = own_pairs[:, 1].reshape(SEQ_G, KVH, HD)
    prompt_pair = lax.dynamic_index_in_dim(prompt_kv, group_index, 0, keepdims=False).astype(jnp.float32)
    prompt_keys = prompt_pair[0].reshape(PROMPT, KVH, HD)
    prompt_values = prompt_pair[1].reshape(PROMPT, KVH, HD)
    suffix_pair = lax.dynamic_slice_in_dim(suffix_kv, first_row, SEQ_G, 0).astype(jnp.float32)
    suffix_keys = suffix_pair[:, 0].reshape(SEQ_G, SUF, KVH, HD)
    suffix_values = suffix_pair[:, 1].reshape(SEQ_G, SUF, KVH, HD)
    seq_lengths = lax.dynamic_slice_in_dim(lengths, first_row, SEQ_G, 0)
    score_scale = HD ** (-0.5)
    prompt_scores = jnp.einsum('skgd,pkd->skgp', query_heads, prompt_keys) * score_scale
    suffix_scores = jnp.einsum('skgd,spkd->skgp', query_heads, suffix_keys) * score_scale
    own_scores = jnp.einsum('skgd,skd->skg', query_heads, own_keys) * score_scale
    live_slots = (jnp.arange(SUF, dtype=jnp.int32)[None, :] < seq_lengths[:, None])[:, None, None, :]
    suffix_scores = jnp.where(live_slots, suffix_scores, neg_big)
    highest = jnp.maximum(jnp.maximum(lax.optimization_barrier(jnp.max(prompt_scores, axis=-1)), lax.optimization_barrier(jnp.max(suffix_scores, axis=-1))), own_scores)
    prompt_weights = jnp.exp(prompt_scores - highest[..., None])
    suffix_weights = jnp.where(live_slots, jnp.exp(suffix_scores - highest[..., None]), 0.0)
    own_weights = jnp.exp(own_scores - highest)
    totals = lax.optimization_barrier(jnp.sum(prompt_weights, axis=-1)) + lax.optimization_barrier(jnp.sum(suffix_weights, axis=-1)) + own_weights
    mixture = jnp.einsum('skgp,pkd->skgd', round_trip(prompt_weights), prompt_values)
    mixture = mixture + jnp.einsum('skgp,spkd->skgd', round_trip(suffix_weights), suffix_values)
    mixture = mixture + round_trip(own_weights)[..., None] * own_values[:, :, None, :]
    return (mixture / totals[..., None]).astype(jnp.bfloat16).reshape(SEQ_G, HEADS * HD)

def reference(hidden, queries, new_kv, prompt_kv, suffix_kv, lengths, w_out, moe_gain, w_router, expert_weights, old_lines, new_lines, routes):

    def one_group(group_index):
        return group_attention(queries, new_kv, prompt_kv, suffix_kv, lengths, group_index)
    attended = lax.map(one_group, jnp.arange(G, dtype=jnp.int32)).reshape(TOKENS, HEADS * HD)
    projected = jnp.dot(attended, w_out, preferred_element_type=jnp.float32)
    h_mid = (hidden.astype(jnp.float32) + projected).astype(jnp.bfloat16)
    h_float = h_mid.astype(jnp.float32)
    scaled = (h_float * moe_gain.astype(jnp.float32)[None, :]).astype(jnp.bfloat16)
    inverse_rms = lax.rsqrt(lax.optimization_barrier(jnp.mean(h_float * h_float, axis=1)) + norm_eps)
    logits = jnp.dot(scaled, w_router, preferred_element_type=jnp.float32) * inverse_rms[:, None]
    selected = jnp.take_along_axis(logits, routes, axis=1)
    gates = jax.nn.softmax(selected, axis=-1)
    expert_ids = jnp.arange(E, dtype=jnp.int32)
    coefficient = lax.optimization_barrier(jnp.sum(jnp.where(routes[:, :, None] == expert_ids[None, None, :], gates[:, :, None], 0.0), axis=1))
    coefficient_rows = jnp.transpose(coefficient)

    def expert_step(running, expert_index):
        lines = lax.dynamic_index_in_dim(expert_weights, expert_index, 0, keepdims=False)
        gate_part = jnp.dot(scaled, jnp.transpose(lines[:, 0, :]), preferred_element_type=jnp.float32) * inverse_rms[:, None]
        up_part = jnp.dot(scaled, jnp.transpose(lines[:, 1, :]), preferred_element_type=jnp.float32) * inverse_rms[:, None]
        activated = (jax.nn.silu(gate_part) * up_part).astype(jnp.bfloat16)
        produced = jnp.dot(activated, lines[:, 2, :], preferred_element_type=jnp.float32)
        weight_col = lax.dynamic_index_in_dim(coefficient_rows, expert_index, 0, keepdims=False)
        return (running + weight_col[:, None] * produced, None)
    mixed, unused_stack = lax.scan(expert_step, jnp.zeros((TOKENS, D), jnp.float32), expert_ids)
    layer_out = h_float + mixed
    positions = jnp.argsort(old_lines, axis=1).astype(jnp.int32)
    source_lines = jnp.take_along_axis(positions, new_lines, axis=1).astype(jnp.int32)
    moved_weights = expert_weights[expert_ids[:, None], source_lines]
    return (layer_out, moved_weights)
```

```python
import functools

import jax
import jax.numpy as jnp
from jax import lax
from jax.experimental import pallas as pl
from jax.experimental.pallas import tpu as pltpu
from jax.sharding import PartitionSpec as P

HD = 128
norm_eps = 1e-06
neg_big = -1e30
f32 = jnp.float32
bf16 = jnp.bfloat16
MESH = pl.DeviceIdType.MESH


def rounded_up(value, step):
    return (value + step - 1) // step * step


def dot_nt(a, b):
    return lax.dot_general(a, b, (((1,), (1,)), ((), ())), preferred_element_type=f32)


def step_kernel(
    row_count,
    col_count,
    lengths_ref,
    hidden_ref,
    queries_ref,
    new_kv_ref,
    prompt_ref,
    suffix_ref,
    w_out_ref,
    gain_ref,
    router_ref,
    lines_ref,
    send_slot_ref,
    take_slot_ref,
    routes_ref,
    layer_ref,
    moved_ref,
    part_out,
    part_in,
    heads_in,
    token_out,
    token_in,
    wide,
    summed_out,
    summed_in,
    act_out,
    act_in,
    down,
    mixed_out,
    mixed_in,
    move_out,
    move_in,
    send_sems,
    recv_sems,
):
    row = lax.axis_index("row")
    col = lax.axis_index("col")
    seqs = hidden_ref.shape[0]
    experts, _, line_count, width = lines_ref.shape
    prompt_rows = prompt_ref.shape[2]
    suffix_rows = suffix_ref.shape[2]
    tokens = seqs * row_count
    share = tokens // col_count
    score_scale = HD ** (-0.5)

    barrier = pltpu.get_barrier_semaphore()

    def greet(axis, me, count):
        def body(k, carry):
            pl.semaphore_signal(
                barrier, inc=1, device_id={axis: lax.rem(me + k, count)}, device_id_type=MESH
            )
            return carry

        lax.fori_loop(1, count, body, 0)

    greet("col", col, col_count)
    greet("row", row, row_count)

    def send(axis, me, count, lane, source, target):
        def body(k, carry):
            peer = lax.rem(me + k, count)
            pltpu.make_async_remote_copy(
                src_ref=source(peer),
                dst_ref=target(k),
                send_sem=send_sems.at[lane],
                recv_sem=recv_sems.at[lane],
                device_id={axis: peer},
                device_id_type=MESH,
            ).start()
            return carry

        lax.fori_loop(1, count, body, 0)

    def wait(count, lane, buffer, sems):
        whole = buffer.at[pl.ds(1, count - 1)]
        pltpu.make_async_copy(whole, whole, sems.at[lane]).wait()

    rows = 2 * seqs
    keys = prompt_rows + seqs * suffix_rows
    row_seq = lax.broadcasted_iota(jnp.int32, (rows, keys), 0) % seqs
    lane = lax.broadcasted_iota(jnp.int32, (rows, keys), 1)
    own_lane = lane - prompt_rows
    filled = jnp.zeros((rows, keys), jnp.int32)
    for s in range(seqs):
        filled = jnp.where(row_seq == s, lengths_ref[s], filled)
    slot = col * suffix_rows + own_lane % suffix_rows
    live = (lane < prompt_rows) | ((own_lane // suffix_rows == row_seq) & (slot < filled))

    def query_rows(start):
        first = queries_ref[:, pl.ds(start, HD)].astype(f32)
        second = queries_ref[:, pl.ds(start + HD, HD)].astype(f32)
        return jnp.concatenate([first, second], axis=0)

    def cached(which, head):
        lanes = slice(head * HD, (head + 1) * HD)
        suffix = suffix_ref[:, which, :, lanes].astype(f32).reshape(seqs * suffix_rows, HD)
        return jnp.concatenate([prompt_ref[0, which, :, lanes], suffix.astype(bf16)], axis=0)

    scores = []
    for head in range(col_count):
        scores.append(
            dot_nt(query_rows(2 * head * HD).astype(bf16), cached(0, head)) * score_scale
        )
    half = lax.broadcasted_iota(jnp.int32, (rows, HD), 1) < HD // 2
    for head in range(col_count):
        score = jnp.where(live, scores[head], neg_big)
        top = jnp.max(score, axis=1, keepdims=True).astype(bf16).astype(f32)
        weights = jnp.where(live, jnp.exp(score - top), 0.0)
        total = jnp.sum(weights, axis=1, keepdims=True)
        mixture = jnp.dot(weights.astype(bf16), cached(1, head), preferred_element_type=f32)
        part_out[head, 0:rows, :] = mixture.astype(bf16)
        part_out[head, rows : 2 * rows, :] = jnp.where(half, top, total).astype(bf16)

    pl.semaphore_wait(barrier, row_count + col_count - 2)
    send("col", col, col_count, 0, lambda peer: part_out.at[peer], lambda k: part_in.at[k])

    per_peer = experts * line_count // row_count
    block = move_out.shape[1]
    flat_lines = jnp.concatenate(
        [lines_ref[:, j].reshape(experts * line_count, width) for j in range(3)], axis=1
    )
    peers_at_once = 4
    chunk = peers_at_once * block
    send_slots = send_slot_ref[...]

    def sort_chunk(at, carry):
        wanted = at * chunk + lax.broadcasted_iota(jnp.int32, (chunk, experts * line_count), 0)
        picks = jnp.where(wanted == send_slots, 1.0, 0.0).astype(bf16)
        sorted_lines = jnp.dot(picks, flat_lines, preferred_element_type=f32).astype(bf16)
        move_out[pl.ds(at * peers_at_once, peers_at_once)] = sorted_lines.reshape(
            peers_at_once, block, 3 * width
        )
        return carry

    lax.fori_loop(0, row_count // peers_at_once, sort_chunk, 0)
    move_in[0] = move_out[row]
    send("row", row, row_count, 6, lambda peer: move_out.at[peer], lambda k: move_in.at[k])

    tail = line_count - 128
    for e in range(experts):
        lanes = slice(e * width, (e + 1) * width)
        wide[0:128, lanes] = lines_ref[e, 0, 0:128, :]
        wide[128:256, lanes] = lines_ref[e, 1, 0:128, :]
        wide[256 : 256 + tail, lanes] = lines_ref[e, 0, 128:line_count, :]
        wide[256 + tail : 256 + 2 * tail, lanes] = lines_ref[e, 1, 128:line_count, :]
        spare = 128 - 2 * tail
        router_row = jnp.broadcast_to(router_ref[e : e + 1, :].astype(f32), (spare, width))
        first = lax.broadcasted_iota(jnp.int32, (spare, width), 0) == 0
        wide[256 + 2 * tail : 384, lanes] = jnp.where(first, router_row, 0.0).astype(bf16)
        gap = jnp.zeros((64 - tail, width), bf16)
        down[e, 0:line_count, :] = lines_ref[e, 2]
        down[e, line_count : 128 + 64, :] = gap
        down[e, 192 : 192 + tail, :] = lines_ref[e, 2, 128:line_count, :]
        down[e, 192 + tail : 256, :] = gap

    part_in[0] = part_out[col]
    wait(col_count, 0, part_in, recv_sems)
    own_query = query_rows(pl.multiple_of(col * 2 * HD, 2 * HD))
    own_pair = new_kv_ref[:, :, pl.ds(pl.multiple_of(col * HD, HD), HD)].astype(f32)
    own_key = jnp.concatenate([own_pair[:, 0, :]] * 2, axis=0)
    own_value = jnp.concatenate([own_pair[:, 1, :]] * 2, axis=0)
    own_score = jnp.sum(own_query * own_key, axis=1, keepdims=True) * score_scale
    stats = part_in[:, rows : 2 * rows, :].astype(f32)
    top = jnp.maximum(jnp.max(stats, axis=0)[:, 0:1], own_score)
    own_weight = jnp.exp(own_score - top)
    mixture = own_weight.astype(bf16).astype(f32) * own_value
    total = jnp.zeros((rows, HD), f32)
    for k in range(col_count):
        factor = jnp.exp(stats[k][:, 0:1] - top)
        total = total + factor * stats[k]
        mixture = mixture + factor * part_in[k, 0:rows, :].astype(f32)
    total = total[:, HD // 2 : HD // 2 + 1] + own_weight
    heads_in[0] = (mixture / total).astype(bf16)
    send("col", col, col_count, 1, lambda peer: heads_in.at[0], lambda k: heads_in.at[k])

    wait(col_count, 1, heads_in, recv_sems)
    projected = jnp.zeros((rows, 2 * width), f32)
    for k in range(col_count):
        head = lax.rem(col + col_count - k, col_count)
        start = pl.multiple_of(head * 2 * HD, 2 * HD)
        pair = jnp.concatenate(
            [w_out_ref[pl.ds(start, HD), :], w_out_ref[pl.ds(start + HD, HD), :]], axis=1
        )
        projected = projected + jnp.dot(heads_in[k], pair, preferred_element_type=f32)
    projected = projected[0:seqs, 0:width] + projected[seqs:rows, width : 2 * width]
    h_float = (hidden_ref[...].astype(f32) + projected).astype(bf16).astype(f32)
    scaled = h_float * gain_ref[...].astype(f32)
    squares = jnp.sum(h_float * h_float, axis=1, keepdims=True)
    high = squares.astype(bf16).astype(f32)
    half = lax.broadcasted_iota(jnp.int32, (seqs, width), 1) < width // 2
    message = jnp.concatenate([scaled, jnp.where(half, high, squares - high)], axis=0).astype(bf16)
    token_out[0] = message
    token_in[row] = message
    send("row", row, row_count, 2, lambda peer: token_out.at[0], lambda k: token_in.at[row])

    routes = [jnp.broadcast_to(routes_ref[:, k : k + 1], (tokens, width)) for k in range(2)]
    wait(row_count, 2, token_in, recv_sems)
    everything = token_in[...].astype(f32)
    every_token = everything[:, 0:seqs, :].reshape(tokens, width)
    every_square = everything[:, seqs : 2 * seqs, :].reshape(tokens, width)
    square = every_square[:, 0:1] + every_square[:, width // 2 : width // 2 + 1]
    square_high = square.astype(bf16).astype(f32)
    token_lane = lax.broadcasted_iota(jnp.int32, (tokens, 128), 1)
    for k in range(2):
        masked = jnp.concatenate(
            [jnp.where(routes[k] == e, every_token, 0.0).astype(bf16) for e in range(experts)],
            axis=1,
        )
        picked = dot_nt(masked, wide[...])
        last = picked[:, 256:384]
        at = 2 * tail
        logit = last[:, at : at + 1]
        logit_high = logit.astype(bf16).astype(f32)
        last = jnp.where(token_lane == at + 1, logit - logit_high, last)
        last = jnp.where(token_lane == at + 2, square_high, last)
        last = jnp.where(token_lane == at + 3, square - square_high, last)
        picked = jnp.concatenate([picked[:, 0:256], last], axis=1)
        summed_out[:, k] = picked.reshape(col_count, share, 384).astype(bf16)
    send("col", col, col_count, 3, lambda peer: summed_out.at[peer], lambda k: summed_in.at[k])

    summed_in[0] = summed_out[col]
    wait(col_count, 3, summed_in, recv_sems)
    sums = jnp.zeros((2, share, 384), f32)
    for k in range(col_count):
        sums = sums + summed_in[k].astype(f32)
    last = sums[:, :, 256:384]
    at = 2 * tail
    square = last[:, :, at + 2 : at + 3] + last[:, :, at + 3 : at + 4]
    inverse_rms = lax.rsqrt(square / (width * col_count) + norm_eps)
    logits = (last[:, :, at : at + 1] + last[:, :, at + 1 : at + 2]) * inverse_rms
    logits = jnp.exp(logits - jnp.max(logits, axis=0, keepdims=True))
    gates = logits / jnp.sum(logits, axis=0, keepdims=True)
    last = last.reshape(2 * share, 128)
    shifted = pltpu.roll(last, 128 - tail, 1).reshape(2, share, 128)
    last = last.reshape(2, share, 128)

    def activated(gate, up):
        gate = gate * inverse_rms
        return gate / (1.0 + jnp.exp(-gate)) * (up * inverse_rms) * gates

    act_first = activated(sums[:, :, 0:128], sums[:, :, 128:256])
    act_last = activated(last, shifted)
    share_lane = lax.broadcasted_iota(jnp.int32, (share, 128), 1)
    second = pltpu.roll(act_last[1], 64, 1)
    ends = jnp.where(
        share_lane < tail,
        act_last[0],
        jnp.where((share_lane >= 64) & (share_lane < 64 + tail), second, 0.0),
    )
    message = jnp.concatenate([act_first[0], act_first[1], ends], axis=0).astype(bf16)
    message = message.reshape(3, share, 128)
    act_out[0] = message
    act_in[col] = message
    send("col", col, col_count, 4, lambda peer: act_out.at[0], lambda k: act_in.at[col])

    wait(col_count, 4, act_in, recv_sems)
    firsts = [act_in[:, k].reshape(tokens, 128).astype(f32) for k in range(2)]
    ends = act_in[:, 2].reshape(tokens, 128).astype(f32)
    end_route = jnp.where(token_lane < 64, routes[0], routes[1])
    mixed = jnp.zeros((tokens, width), f32)
    for e in range(experts):
        begin = jnp.where(routes[0] == e, firsts[0], jnp.where(routes[1] == e, firsts[1], 0.0))
        end = jnp.where(end_route == e, ends, 0.0)
        both = jnp.concatenate([begin, end], axis=1).astype(bf16)
        mixed = mixed + jnp.dot(both, down[e], preferred_element_type=f32)
    mixed_out[...] = mixed.reshape(row_count, seqs, width).astype(bf16)
    send("row", row, row_count, 5, lambda peer: mixed_out.at[peer], lambda k: mixed_in.at[k])
    mixed_in[0] = mixed_out[row]
    wait(row_count, 5, mixed_in, recv_sems)
    layer_ref[...] = h_float + jnp.sum(mixed_in[...].astype(f32), axis=0)

    wait(row_count, 6, move_in, recv_sems)
    everything = move_in[...].reshape(row_count * block, 3 * width)

    def place(e, carry):
        slots = take_slot_ref[pl.ds(pl.multiple_of(e * line_count, line_count), line_count), :]
        held = lax.broadcasted_iota(jnp.int32, (line_count, row_count * block), 1)
        picks = jnp.where(held == slots, 1.0, 0.0).astype(bf16)
        placed = jnp.dot(picks, everything, preferred_element_type=f32).astype(bf16)
        for j in range(3):
            moved_ref[e, j] = placed[:, j * width : (j + 1) * width]
        return carry

    lax.fori_loop(0, experts, place, 0)

    wait(col_count, 0, part_in, send_sems)
    wait(col_count, 1, heads_in, send_sems)
    wait(row_count, 2, token_in, send_sems)
    wait(col_count, 3, summed_in, send_sems)
    wait(col_count, 4, act_in, send_sems)
    wait(row_count, 5, mixed_in, send_sems)
    wait(row_count, 6, move_in, send_sems)


def owner_slots(ids, table, block, per_peer):
    experts, full = table.shape
    lines = ids.shape[1]
    owners = jnp.arange(full, dtype=jnp.int32) // lines
    owner = jnp.sum(
        jnp.where(ids[:, :, None] == table[:, None, :], owners[None, None, :], 0), axis=2
    )
    keys = owner * (experts * full) + jnp.arange(experts, dtype=jnp.int32)[:, None] * full + ids
    owner, keys = owner.reshape(-1), keys.reshape(-1)
    place = jnp.sum((keys[None, :] < keys[:, None]).astype(jnp.int32), axis=1)
    return owner, place + owner * (block - per_peer)


def local(
    row_count,
    col_count,
    hidden,
    queries,
    new_kv,
    prompt_kv,
    suffix_kv,
    lengths,
    w_out,
    moe_gain,
    w_router,
    expert_weights,
    old_lines,
    new_lines,
    routes,
):
    experts, line_count, parts, width = expert_weights.shape
    seqs = hidden.shape[0]
    tokens = seqs * row_count
    share = tokens // col_count
    per_peer = experts * line_count // row_count
    block = rounded_up(per_peer, 16)
    row = lax.axis_index("row")
    held = lax.dynamic_slice_in_dim(old_lines, row * line_count, line_count, 1)
    wanted = lax.dynamic_slice_in_dim(new_lines, row * line_count, line_count, 1)
    _, send_slots = owner_slots(held, new_lines, block, per_peer)
    source, place = owner_slots(wanted, old_lines, block, per_peer)
    distance = lax.rem(row + row_count - source, row_count)
    take_slots = place + (distance - source) * block
    vmem = pl.BlockSpec(memory_space=pltpu.VMEM)
    rows = 2 * seqs
    layer_out, moved = pl.pallas_call(
        functools.partial(step_kernel, row_count, col_count),
        out_shape=(
            jax.ShapeDtypeStruct((seqs, width), f32),
            jax.ShapeDtypeStruct((experts, parts, line_count, width), bf16),
        ),
        in_specs=[pl.BlockSpec(memory_space=pltpu.SMEM)] + [vmem] * 12,
        out_specs=(vmem, vmem),
        scratch_shapes=[
            pltpu.VMEM((col_count, 2 * rows, HD), bf16),
            pltpu.VMEM((col_count, 2 * rows, HD), bf16),
            pltpu.VMEM((col_count, rows, HD), bf16),
            pltpu.VMEM((1, rows, width), bf16),
            pltpu.VMEM((row_count, rows, width), bf16),
            pltpu.VMEM((384, experts * width), bf16),
            pltpu.VMEM((col_count, 2, share, 384), bf16),
            pltpu.VMEM((col_count, 2, share, 384), bf16),
            pltpu.VMEM((1, 3, share, 128), bf16),
            pltpu.VMEM((col_count, 3, share, 128), bf16),
            pltpu.VMEM((experts, 256, width), bf16),
            pltpu.VMEM((row_count, seqs, width), bf16),
            pltpu.VMEM((row_count, seqs, width), bf16),
            pltpu.VMEM((row_count, block, parts * width), bf16),
            pltpu.VMEM((row_count, block, parts * width), bf16),
            pltpu.SemaphoreType.DMA((7,)),
            pltpu.SemaphoreType.DMA((7,)),
        ],
        compiler_params=pltpu.CompilerParams(
            collective_id=0, has_side_effects=True, vmem_limit_bytes=56 << 20
        ),
        name="decode_step",
    )(
        lengths,
        hidden,
        queries,
        new_kv,
        prompt_kv,
        suffix_kv,
        w_out,
        moe_gain.reshape(1, width),
        jnp.transpose(w_router),
        jnp.transpose(expert_weights, (0, 2, 1, 3)),
        send_slots.reshape(1, -1),
        take_slots.reshape(-1, 1),
        routes,
    )
    return layer_out, jnp.transpose(moved, (0, 2, 1, 3))


def solution(mesh):
    return jax.shard_map(
        functools.partial(local, mesh.shape["row"], mesh.shape["col"]),
        mesh=mesh,
        in_specs=(
            P("row", "col"),
            P("row", None),
            P("row", None, None),
            P("row", None, "col", None),
            P("row", None, "col", None),
            P("row"),
            P(None, "col"),
            P("col"),
            P("col", None),
            P(None, "row", None, "col"),
            P(),
            P(),
            P(),
        ),
        out_specs=(P("row", "col"), P(None, "row", None, "col")),
        check_vma=False,
    )
```

```python
import functools

import jax
import jax.numpy as jnp
from jax import lax
from jax.experimental import pallas as pl
from jax.experimental.pallas import tpu as pltpu
from jax.sharding import PartitionSpec as P

HD = 128
norm_eps = 1e-06
neg_big = -1e30
f32 = jnp.float32
bf16 = jnp.bfloat16
MESH = pl.DeviceIdType.MESH
MOVES = (0, 3, 6, 9, 12, 15, 18, 21, 24, 27, 29, 31)


def rounded_up(value, step):
    return (value + step - 1) // step * step


def dot_nt(a, b):
    return lax.dot_general(a, b, (((1,), (1,)), ((), ())), preferred_element_type=f32)


def split(count):
    far = 4 if count >= 16 else 2
    return far, count // far


def line_slots(row, row_count, block, ids_ref, table_ref, line_count, outgoing):
    experts, full = table_ref.shape
    window = min(full, 512)
    start = row * line_count
    base = jnp.minimum(start // 128 * 128, full - window)
    held = ids_ref[:, pl.ds(pl.multiple_of(base, 128), window)]
    held = pltpu.roll(held, lax.rem(window - (start - base), window), 1)[:, 0:256]
    id_rows = held.astype(f32)
    padded = jnp.concatenate([id_rows, jnp.zeros((128 - experts, 256), f32)], axis=0)
    id_columns = jnp.transpose(padded)[0:line_count]
    owner_lane = lax.broadcasted_iota(jnp.int32, (1, 128), 1)
    owners_f32 = owner_lane.astype(f32)
    if outgoing:
        offsets = owners_f32 * block
    else:
        far_count, near_count = split(row_count)
        far = lax.rem(row // near_count - owner_lane // near_count + 128 * far_count, far_count)
        near = lax.rem(row % near_count - owner_lane % near_count + near_count, near_count)
        offsets = (near * far_count + far).astype(f32) * block
    counts = jnp.zeros((1, 128), f32)
    slots = []
    for e in range(experts):
        id_column = id_columns[:, e : e + 1]
        wanted = jnp.broadcast_to(id_column, (line_count, 128)).astype(jnp.int32)

        def search(chunk, found):
            at = chunk * 128
            table = table_ref[e : e + 1, pl.ds(pl.multiple_of(at, 128), 128)]
            first = at // line_count
            owner = first + jnp.where(owner_lane + at >= (first + 1) * line_count, 1, 0)
            return jnp.where(wanted == table, owner, found)

        found = lax.fori_loop(
            0, full // 128, search, jnp.zeros((line_count, 128), jnp.int32), unroll=4
        )
        owner_column = jnp.sum(found.astype(f32), axis=1, keepdims=True)
        hits = jnp.where(owner_column == owners_f32, 1.0, 0.0)
        pack = jnp.concatenate([counts, offsets, owners_f32, jnp.zeros((5, 128), f32)], axis=0)
        looked = dot_nt(pack.astype(bf16), hits.astype(bf16))
        owner_row = looked[2:3]
        id_row = id_rows[e : e + 1, 0:line_count]
        same = owner_column == owner_row
        if outgoing:
            rank = jnp.sum(jnp.where(same & (id_column < id_row), 1.0, 0.0), axis=0, keepdims=True)
            slots.append(rank + looked[0:1] + looked[1:2])
        else:
            rank = jnp.sum(jnp.where(same & (id_row < id_column), 1.0, 0.0), axis=1, keepdims=True)
            slots.append(rank + jnp.sum(hits * (counts + offsets), axis=1, keepdims=True))
        counts = counts + jnp.sum(hits, axis=0, keepdims=True)
    return slots


def step_kernel(
    row_count,
    col_count,
    lengths_ref,
    hidden_ref,
    queries_ref,
    new_kv_ref,
    prompt_ref,
    suffix_ref,
    w_out_ref,
    gain_ref,
    router_ref,
    lines_ref,
    old_lines_ref,
    new_lines_ref,
    routes_ref,
    layer_ref,
    moved_ref,
    part_out,
    part_in,
    joined_out,
    joined_in,
    heads_in,
    token_in,
    wide,
    summed_out,
    summed_in,
    halved_out,
    halved_in,
    act_in,
    down,
    mixed_out,
    mixed_in,
    nearer_out,
    nearer_in,
    move_out,
    move_in,
    take_slots,
    send_sems,
    recv_sems,
):
    row = lax.axis_index("row")
    col = lax.axis_index("col")
    seqs = hidden_ref.shape[0]
    experts, _, line_count, width = lines_ref.shape
    prompt_rows = prompt_ref.shape[2]
    suffix_rows = suffix_ref.shape[2]
    tokens = seqs * row_count
    share = tokens // col_count
    score_scale = HD ** (-0.5)

    barrier = pltpu.get_barrier_semaphore()
    row_far_count, row_near_count = split(row_count)
    col_far_count, col_near_count = split(col_count)
    row_far, row_near = row // row_near_count, row % row_near_count
    col_far, col_near = col // col_near_count, col % col_near_count

    def col_far_peer(k):
        far = lax.rem(col_far + k, col_far_count)
        return far, {"col": far * col_near_count + col_near}

    def col_near_peer(k):
        near = lax.rem(col_near + k, col_near_count)
        return near, {"col": col_far * col_near_count + near}

    def row_far_peer(k):
        far = lax.rem(row_far + k, row_far_count)
        return far, {"row": far * row_near_count + row_near}

    def row_near_peer(k):
        near = lax.rem(row_near + k, row_near_count)
        return near, {"row": row_far * row_near_count + near}

    def row_peer(k):
        far = lax.rem(row_far + k % row_far_count, row_far_count)
        near = lax.rem(row_near + k // row_far_count, row_near_count)
        peer = far * row_near_count + near
        return peer, {"row": peer}

    def greet(peer_of, count):
        def body(k, carry):
            pl.semaphore_signal(barrier, inc=1, device_id=peer_of(k)[1], device_id_type=MESH)
            return carry

        lax.fori_loop(1, count, body, 0)

    greet(col_far_peer, col_far_count)
    greet(col_near_peer, col_near_count)
    greet(row_peer, row_count)
    greeted = col_far_count + col_near_count + row_count - 3

    def send(peer_of, first, last, lane, source, target):
        def body(k, carry):
            peer, device = peer_of(k)
            pltpu.make_async_remote_copy(
                src_ref=source(peer),
                dst_ref=target(k),
                send_sem=send_sems.at[lane],
                recv_sem=recv_sems.at[lane],
                device_id=device,
                device_id_type=MESH,
            ).start()
            return carry

        lax.fori_loop(first, last, body, 0)

    def wait(lane, copies, sems):
        pltpu.make_async_copy(copies, copies, sems.at[lane]).wait()

    rows = 2 * seqs
    keys = prompt_rows + seqs * suffix_rows
    row_seq = lax.broadcasted_iota(jnp.int32, (rows, keys), 0) % seqs
    lane = lax.broadcasted_iota(jnp.int32, (rows, keys), 1)
    own_lane = lane - prompt_rows
    filled = jnp.zeros((rows, keys), jnp.int32)
    for s in range(seqs):
        filled = jnp.where(row_seq == s, lengths_ref[s], filled)
    slot = col * suffix_rows + own_lane % suffix_rows
    live = (lane < prompt_rows) | ((own_lane // suffix_rows == row_seq) & (slot < filled))

    def query_rows(start):
        first = queries_ref[:, pl.ds(start, HD)].astype(f32)
        second = queries_ref[:, pl.ds(start + HD, HD)].astype(f32)
        return jnp.concatenate([first, second], axis=0)

    def cached(which, head):
        lanes = slice(head * HD, (head + 1) * HD)
        suffix = suffix_ref[:, which, :, lanes].astype(f32).reshape(seqs * suffix_rows, HD)
        return jnp.concatenate([prompt_ref[0, which, :, lanes], suffix.astype(bf16)], axis=0)

    scores = []
    for head in range(col_count):
        scores.append(
            dot_nt(query_rows(2 * head * HD).astype(bf16), cached(0, head)) * score_scale
        )
    half = lax.broadcasted_iota(jnp.int32, (rows, HD), 1) < HD // 2
    for head in range(col_count):
        score = jnp.where(live, scores[head], neg_big)
        top = jnp.max(score, axis=1, keepdims=True).astype(bf16).astype(f32)
        weights = jnp.where(live, jnp.exp(score - top), 0.0)
        total = jnp.sum(weights, axis=1, keepdims=True)
        mixture = jnp.dot(weights.astype(bf16), cached(1, head), preferred_element_type=f32)
        near, far = head % col_near_count, head // col_near_count
        part_out[near, far, 0:rows, :] = mixture.astype(bf16)
        part_out[near, far, rows : 2 * rows, :] = jnp.where(half, top, total).astype(bf16)

    pl.semaphore_wait(barrier, greeted)
    near_parts = part_in.at[pl.ds(1, col_near_count - 1)]
    send(
        col_near_peer,
        1,
        col_near_count,
        0,
        lambda peer: part_out.at[peer],
        lambda k: part_in.at[k],
    )

    per_peer = experts * line_count // row_count
    block = move_out.shape[1]
    slots = line_slots(row, row_count, block, old_lines_ref, new_lines_ref, line_count, True)
    peers_at_once = 4
    chunk = peers_at_once * block

    def sort_chunk(at, carry):
        wanted = (
            at * chunk + lax.broadcasted_iota(jnp.int32, (chunk, line_count), 0)
        ).astype(f32)
        sorted_lines = jnp.zeros((chunk, 3 * width), f32)
        for e in range(experts):
            picks = jnp.where(wanted == slots[e], 1.0, 0.0).astype(bf16)
            lines = jnp.concatenate([lines_ref[e, j] for j in range(3)], axis=1)
            sorted_lines = sorted_lines + jnp.dot(picks, lines, preferred_element_type=f32)
        move_out[pl.ds(at * peers_at_once, peers_at_once)] = (
            sorted_lines.astype(bf16).reshape(peers_at_once, block, 3 * width)
        )
        return carry

    moves = [1 + (row_count - 1) * share_of // 31 for share_of in MOVES]

    def move(batch):
        send(
            row_peer,
            moves[batch],
            moves[batch + 1],
            12,
            lambda peer: move_out.at[peer],
            lambda k: move_in.at[k],
        )

    def join(parts, tops):
        top = tops[0]
        for other in tops[1:]:
            top = jnp.maximum(top, other)
        total = jnp.zeros((rows, HD), f32)
        mixture = jnp.zeros((rows, HD), f32)
        for part in parts:
            stats = part[rows : 2 * rows].astype(f32)
            factor = jnp.exp(stats[:, 0:1] - top)
            total = total + factor * stats
            mixture = mixture + factor * part[0:rows].astype(f32)
        return top, total[:, HD // 2 : HD // 2 + 1], mixture

    def top_of(part):
        return part[rows : 2 * rows].astype(f32)[:, 0:1]

    part_in[0] = part_out[col_near]
    wait(0, near_parts, recv_sems)
    for far in range(col_far_count):
        parts = [part_in[k, far] for k in range(col_near_count)]
        top, total, mixture = join(parts, [top_of(part) for part in parts])
        joined_out[far, 0:rows, :] = mixture.astype(bf16)
        joined_out[far, rows : 2 * rows, :] = jnp.where(half, top, total).astype(bf16)
    far_parts = joined_in.at[pl.ds(1, col_far_count - 1)]
    send(
        col_far_peer,
        1,
        col_far_count,
        1,
        lambda peer: joined_out.at[peer],
        lambda k: joined_in.at[k],
    )
    lax.fori_loop(0, row_count // peers_at_once, sort_chunk, 0)
    move_in[0] = move_out[row]
    move(0)

    joined_in[0] = joined_out[col_far]
    own_query = query_rows(pl.multiple_of(col * 2 * HD, 2 * HD))
    own_pair = new_kv_ref[:, :, pl.ds(pl.multiple_of(col * HD, HD), HD)].astype(f32)
    own_key = jnp.concatenate([own_pair[:, 0, :]] * 2, axis=0)
    own_value = jnp.concatenate([own_pair[:, 1, :]] * 2, axis=0)
    own_score = jnp.sum(own_query * own_key, axis=1, keepdims=True) * score_scale
    wait(1, far_parts, recv_sems)
    parts = [joined_in[k] for k in range(col_far_count)]
    top, total, mixture = join(parts, [top_of(part) for part in parts] + [own_score])
    own_weight = jnp.exp(own_score - top)
    mixture = mixture + own_weight.astype(bf16).astype(f32) * own_value
    heads_in[0, col_far] = (mixture / (total + own_weight)).astype(bf16)
    own_heads = heads_in.at[0, col_far]
    far_heads = heads_in.at[0, pl.ds(0, col_far_count - 1)]
    near_heads = heads_in.at[pl.ds(1, col_near_count - 1)]
    send(col_far_peer, 1, col_far_count, 2, lambda peer: own_heads, lambda k: own_heads)
    move(1)

    tail = line_count - 128
    for e in range(experts):
        lanes = slice(e * width, (e + 1) * width)
        wide[0:128, lanes] = lines_ref[e, 0, 0:128, :]
        wide[128:256, lanes] = lines_ref[e, 1, 0:128, :]
        wide[256 : 256 + tail, lanes] = lines_ref[e, 0, 128:line_count, :]
        wide[256 + tail : 256 + 2 * tail, lanes] = lines_ref[e, 1, 128:line_count, :]
        spare = 128 - 2 * tail
        router_row = jnp.broadcast_to(router_ref[e : e + 1, :].astype(f32), (spare, width))
        first = lax.broadcasted_iota(jnp.int32, (spare, width), 0) == 0
        wide[256 + 2 * tail : 384, lanes] = jnp.where(first, router_row, 0.0).astype(bf16)
        gap = jnp.zeros((64 - tail, width), bf16)
        down[e, 0:line_count, :] = lines_ref[e, 2]
        down[e, line_count : 128 + 64, :] = gap
        down[e, 192 : 192 + tail, :] = lines_ref[e, 2, 128:line_count, :]
        down[e, 192 + tail : 256, :] = gap

    wait(2, far_heads, recv_sems)
    send(
        col_near_peer,
        1,
        col_near_count,
        3,
        lambda peer: heads_in.at[0],
        lambda k: heads_in.at[k],
    )
    move(2)
    wait(3, near_heads, recv_sems)
    projected = jnp.zeros((rows, 2 * width), f32)
    for k in range(col_near_count):
        near = lax.rem(col_near + col_near_count - k, col_near_count)
        for far in range(col_far_count):
            head = far * col_near_count + near
            start = pl.multiple_of(head * 2 * HD, 2 * HD)
            pair = jnp.concatenate(
                [w_out_ref[pl.ds(start, HD), :], w_out_ref[pl.ds(start + HD, HD), :]], axis=1
            )
            projected = projected + jnp.dot(heads_in[k, far], pair, preferred_element_type=f32)
    projected = projected[0:seqs, 0:width] + projected[seqs:rows, width : 2 * width]
    h_float = (hidden_ref[...].astype(f32) + projected).astype(bf16).astype(f32)
    scaled = h_float * gain_ref[...].astype(f32)
    squares = jnp.sum(h_float * h_float, axis=1, keepdims=True)
    high = squares.astype(bf16).astype(f32)
    half = lax.broadcasted_iota(jnp.int32, (seqs, width), 1) < width // 2
    message = jnp.concatenate([scaled, jnp.where(half, high, squares - high)], axis=0).astype(bf16)
    token_in[row_near, row_far] = message
    own_tokens = token_in.at[row_near, row_far]
    far_tokens = token_in.at[0, pl.ds(0, row_far_count - 1)]
    near_tokens = token_in.at[pl.ds(0, row_near_count - 1)]
    send(row_far_peer, 1, row_far_count, 4, lambda peer: own_tokens, lambda k: own_tokens)
    move(3)

    for e, slots in enumerate(
        line_slots(row, row_count, block, new_lines_ref, old_lines_ref, line_count, False)
    ):
        take_slots[e] = jnp.broadcast_to(slots, (line_count, 128))
    routes = [
        jnp.transpose(jnp.broadcast_to(routes_ref[k : k + 1, :].astype(f32), (width, tokens)))
        for k in range(2)
    ]

    wait(4, far_tokens, recv_sems)
    own_tokens = token_in.at[row_near]
    send(row_near_peer, 1, row_near_count, 5, lambda peer: own_tokens, lambda k: own_tokens)
    move(4)
    wait(5, near_tokens, recv_sems)
    everything = token_in[...].astype(f32)
    by_row = [everything[r % row_near_count, r // row_near_count] for r in range(row_count)]
    every_token = jnp.concatenate([part[0:seqs] for part in by_row], axis=0)
    every_square = jnp.concatenate([part[seqs : 2 * seqs] for part in by_row], axis=0)
    square = every_square[:, 0:1] + every_square[:, width // 2 : width // 2 + 1]
    token_lane = lax.broadcasted_iota(jnp.int32, (tokens, 128), 1)
    at = 2 * tail

    def with_spares(last, logit, square):
        spare = lax.broadcasted_iota(jnp.int32, last.shape, len(last.shape) - 1) - at
        logit_high = logit.astype(bf16).astype(f32)
        square_high = square.astype(bf16).astype(f32)
        last = jnp.where(spare == 0, logit_high, last)
        last = jnp.where(spare == 1, logit - logit_high, last)
        last = jnp.where(spare == 2, square_high, last)
        return jnp.where(spare == 3, square - square_high, last)

    for k in range(2):
        masked = jnp.concatenate(
            [jnp.where(routes[k] == e, every_token, 0.0).astype(bf16) for e in range(experts)],
            axis=1,
        )
        picked = dot_nt(masked, wide[...])
        last = picked[:, 256:384]
        last = with_spares(last, last[:, at : at + 1], square)
        picked = jnp.concatenate([picked[:, 0:256], last], axis=1).astype(bf16)
        for c in range(col_count):
            summed_out[c % col_near_count, c // col_near_count, k] = picked[
                c * share : (c + 1) * share
            ]
    near_sums = summed_in.at[pl.ds(1, col_near_count - 1)]
    far_sums = halved_in.at[pl.ds(1, col_far_count - 1)]
    send(
        col_near_peer,
        1,
        col_near_count,
        6,
        lambda peer: summed_out.at[peer],
        lambda k: summed_in.at[k],
    )
    move(5)

    summed_in[0] = summed_out[col_near]
    wait(6, near_sums, recv_sems)
    for far in range(col_far_count):
        sums = summed_in[0, far].astype(f32)
        for k in range(1, col_near_count):
            sums = sums + summed_in[k, far].astype(f32)
        last = sums[:, :, 256:384]
        logit = last[:, :, at : at + 1] + last[:, :, at + 1 : at + 2]
        square = last[:, :, at + 2 : at + 3] + last[:, :, at + 3 : at + 4]
        halved_out[far, :, :, 0:256] = sums[:, :, 0:256].astype(bf16)
        halved_out[far, :, :, 256:384] = with_spares(last, logit, square).astype(bf16)
    send(
        col_far_peer,
        1,
        col_far_count,
        7,
        lambda peer: halved_out.at[peer],
        lambda k: halved_in.at[k],
    )
    move(6)
    halved_in[0] = halved_out[col_far]
    wait(7, far_sums, recv_sems)
    sums = halved_in[0].astype(f32)
    for k in range(1, col_far_count):
        sums = sums + halved_in[k].astype(f32)
    last = sums[:, :, 256:384]
    square = last[:, :, at + 2 : at + 3] + last[:, :, at + 3 : at + 4]
    inverse_rms = lax.rsqrt(square / (width * col_count) + norm_eps)
    logits = (last[:, :, at : at + 1] + last[:, :, at + 1 : at + 2]) * inverse_rms
    logits = jnp.exp(logits - jnp.max(logits, axis=0, keepdims=True))
    gates = logits / jnp.sum(logits, axis=0, keepdims=True)
    last = last.reshape(2 * share, 128)
    shifted = pltpu.roll(last, 128 - tail, 1).reshape(2, share, 128)
    last = last.reshape(2, share, 128)

    def activated(gate, up):
        gate = gate * inverse_rms
        return gate / (1.0 + jnp.exp(-gate)) * (up * inverse_rms) * gates

    act_first = activated(sums[:, :, 0:128], sums[:, :, 128:256])
    act_last = activated(last, shifted)
    share_lane = lax.broadcasted_iota(jnp.int32, (share, 128), 1)
    second = pltpu.roll(act_last[1], 64, 1)
    ends = jnp.where(
        share_lane < tail,
        act_last[0],
        jnp.where((share_lane >= 64) & (share_lane < 64 + tail), second, 0.0),
    )
    message = jnp.concatenate([act_first[0], act_first[1], ends], axis=0).astype(bf16)
    act_in[col_near, col_far] = message.reshape(3, share, 128)
    own_acts = act_in.at[col_near, col_far]
    far_acts = act_in.at[0, pl.ds(0, col_far_count - 1)]
    near_acts = act_in.at[pl.ds(0, col_near_count - 1)]
    send(col_far_peer, 1, col_far_count, 8, lambda peer: own_acts, lambda k: own_acts)
    move(7)
    wait(8, far_acts, recv_sems)
    own_row = act_in.at[col_near]
    send(col_near_peer, 1, col_near_count, 9, lambda peer: own_row, lambda k: own_row)
    move(8)

    wait(9, near_acts, recv_sems)
    by_col = [act_in[c % col_near_count, c // col_near_count] for c in range(col_count)]
    firsts = [
        jnp.concatenate([part[k] for part in by_col], axis=0).astype(f32) for k in range(2)
    ]
    ends = jnp.concatenate([part[2] for part in by_col], axis=0).astype(f32)
    end_route = jnp.where(token_lane < 64, routes[0], routes[1])
    mixed = jnp.zeros((tokens, width), f32)
    for e in range(experts):
        begin = jnp.where(routes[0] == e, firsts[0], jnp.where(routes[1] == e, firsts[1], 0.0))
        end = jnp.where(end_route == e, ends, 0.0)
        both = jnp.concatenate([begin, end], axis=1).astype(bf16)
        mixed = mixed + jnp.dot(both, down[e], preferred_element_type=f32)
    for r in range(row_count):
        mixed_out[r % row_near_count, r // row_near_count] = mixed[
            r * seqs : (r + 1) * seqs
        ].astype(bf16)
    near_mixed = mixed_in.at[pl.ds(1, row_near_count - 1)]
    far_mixed = nearer_in.at[pl.ds(1, row_far_count - 1)]
    send(
        row_near_peer,
        1,
        row_near_count,
        10,
        lambda peer: mixed_out.at[peer],
        lambda k: mixed_in.at[k],
    )
    move(9)
    mixed_in[0] = mixed_out[row_near]
    wait(10, near_mixed, recv_sems)
    nearer_out[...] = jnp.sum(mixed_in[...].astype(f32), axis=0).astype(bf16)
    send(
        row_far_peer,
        1,
        row_far_count,
        11,
        lambda peer: nearer_out.at[peer],
        lambda k: nearer_in.at[k],
    )
    move(10)
    nearer_in[0] = nearer_out[row_far]
    wait(11, far_mixed, recv_sems)
    layer_ref[...] = h_float + jnp.sum(nearer_in[...].astype(f32), axis=0)

    moved = move_in.at[pl.ds(1, row_count - 1)]
    wait(12, moved, recv_sems)
    everything = move_in[...].reshape(row_count * block, 3 * width)

    def place(e, carry):
        slots = take_slots[e][:, 0:1]
        held = lax.broadcasted_iota(jnp.int32, (line_count, row_count * block), 1).astype(f32)
        picks = jnp.where(held == slots, 1.0, 0.0).astype(bf16)
        placed = jnp.dot(picks, everything, preferred_element_type=f32).astype(bf16)
        for j in range(3):
            moved_ref[e, j] = placed[:, j * width : (j + 1) * width]
        return carry

    lax.fori_loop(0, experts, place, 0)

    sent = [near_parts, far_parts, far_heads, near_heads, far_tokens, near_tokens, near_sums]
    sent += [far_sums, far_acts, near_acts, near_mixed, far_mixed, moved]
    for lane, copies in enumerate(sent):
        wait(lane, copies, send_sems)


def local(
    row_count,
    col_count,
    hidden,
    queries,
    new_kv,
    prompt_kv,
    suffix_kv,
    lengths,
    w_out,
    moe_gain,
    w_router,
    expert_weights,
    old_lines,
    new_lines,
    routes,
):
    experts, line_count, parts, width = expert_weights.shape
    seqs = hidden.shape[0]
    tokens = seqs * row_count
    share = tokens // col_count
    per_peer = experts * line_count // row_count
    block = rounded_up(per_peer, 16)
    row_far, row_near = split(row_count)
    col_far, col_near = split(col_count)
    vmem = pl.BlockSpec(memory_space=pltpu.VMEM)
    rows = 2 * seqs
    layer_out, moved = pl.pallas_call(
        functools.partial(step_kernel, row_count, col_count),
        out_shape=(
            jax.ShapeDtypeStruct((seqs, width), f32),
            jax.ShapeDtypeStruct((experts, parts, line_count, width), bf16),
        ),
        in_specs=[pl.BlockSpec(memory_space=pltpu.SMEM)] + [vmem] * 12,
        out_specs=(vmem, vmem),
        scratch_shapes=[
            pltpu.VMEM((col_near, col_far, 2 * rows, HD), bf16),
            pltpu.VMEM((col_near, col_far, 2 * rows, HD), bf16),
            pltpu.VMEM((col_far, 2 * rows, HD), bf16),
            pltpu.VMEM((col_far, 2 * rows, HD), bf16),
            pltpu.VMEM((col_near, col_far, rows, HD), bf16),
            pltpu.VMEM((row_near, row_far, rows, width), bf16),
            pltpu.VMEM((384, experts * width), bf16),
            pltpu.VMEM((col_near, col_far, 2, share, 384), bf16),
            pltpu.VMEM((col_near, col_far, 2, share, 384), bf16),
            pltpu.VMEM((col_far, 2, share, 384), bf16),
            pltpu.VMEM((col_far, 2, share, 384), bf16),
            pltpu.VMEM((col_near, col_far, 3, share, 128), bf16),
            pltpu.VMEM((experts, 256, width), bf16),
            pltpu.VMEM((row_near, row_far, seqs, width), bf16),
            pltpu.VMEM((row_near, row_far, seqs, width), bf16),
            pltpu.VMEM((row_far, seqs, width), bf16),
            pltpu.VMEM((row_far, seqs, width), bf16),
            pltpu.VMEM((row_count, block, parts * width), bf16),
            pltpu.VMEM((row_count, block, parts * width), bf16),
            pltpu.VMEM((experts, line_count, 128), f32),
            pltpu.SemaphoreType.DMA((13,)),
            pltpu.SemaphoreType.DMA((13,)),
        ],
        compiler_params=pltpu.CompilerParams(
            collective_id=0, has_side_effects=True, vmem_limit_bytes=56 << 20
        ),
        name="decode_step",
    )(
        lengths,
        hidden,
        queries,
        new_kv,
        prompt_kv,
        suffix_kv,
        w_out,
        moe_gain.reshape(1, width),
        jnp.transpose(w_router),
        jnp.transpose(expert_weights, (0, 2, 1, 3)),
        old_lines,
        new_lines,
        jnp.transpose(routes),
    )
    return layer_out, jnp.transpose(moved, (0, 2, 1, 3))


def solution(mesh):
    return jax.shard_map(
        functools.partial(local, mesh.shape["row"], mesh.shape["col"]),
        mesh=mesh,
        in_specs=(
            P("row", "col"),
            P("row", None),
            P("row", None, None),
            P("row", None, "col", None),
            P("row", None, "col", None),
            P("row"),
            P(None, "col"),
            P("col"),
            P("col", None),
            P(None, "row", None, "col"),
            P(),
            P(),
            P(),
        ),
        out_specs=(P("row", "col"), P(None, "row", None, "col")),
        check_vma=False,
    )
```

```python
import functools

import jax
import jax.numpy as jnp
from jax import lax
from jax.experimental import pallas as pl
from jax.experimental.pallas import tpu as pltpu
from jax.sharding import PartitionSpec as P

HD = 128
norm_eps = 1e-06
neg_big = -1e30
f32 = jnp.float32
bf16 = jnp.bfloat16
i16 = jnp.int16
MESH = pl.DeviceIdType.MESH
MOVES = (0, 2, 5, 7, 10, 12, 15, 17, 20, 23, 27, 31)


def rounded_up(value, step):
    return (value + step - 1) // step * step


def dot_nt(a, b):
    return lax.dot_general(a, b, (((1,), (1,)), ((), ())), preferred_element_type=f32)


def split(count):
    far = 4 if count >= 16 else 2
    return far, count // far


def line_slots(row, row_count, block, ids_ref, table_ref, line_count, outgoing):
    experts, full = table_ref.shape
    window = min(full, 512)
    start = row * line_count
    base = jnp.minimum(start // 128 * 128, full - window)
    held = ids_ref[:, pl.ds(pl.multiple_of(base, 128), window)]
    held = pltpu.roll(held, lax.rem(window - (start - base), window), 1)[:, 0:256]
    id_rows = held.astype(f32)
    padded = jnp.concatenate([id_rows, jnp.zeros((128 - experts, 256), f32)], axis=0)
    id_columns = jnp.transpose(padded)[0:line_count]
    owner_lane = lax.broadcasted_iota(jnp.int32, (1, 128), 1)
    owners_f32 = owner_lane.astype(f32)
    if outgoing:
        offsets = owners_f32 * block
    else:
        far_count, near_count = split(row_count)
        far = lax.rem(row // near_count - owner_lane // near_count + 128 * far_count, far_count)
        near = lax.rem(row % near_count - owner_lane % near_count + near_count, near_count)
        offsets = (near * far_count + far).astype(f32) * block
    tiles = line_count // 16
    wanted = [
        jnp.broadcast_to(id_columns[:, e : e + 1], (line_count, 128))
        .astype(jnp.int32)
        .astype(i16)
        .reshape(tiles, 16, 128)
        for e in range(experts)
    ]

    def rows16(row):
        return jnp.broadcast_to(row, (16, 128)).astype(i16)[None]

    found = []
    for e in range(0, experts, 2):

        def search(chunk, both):
            at = chunk * 128
            first = at // line_count
            owner = rows16(first + jnp.where(owner_lane + at >= (first + 1) * line_count, 1, 0))
            return tuple(
                jnp.where(
                    wanted[e + i]
                    == rows16(
                        table_ref[e + i : e + i + 1, pl.ds(pl.multiple_of(at, 128), 128)]
                    ),
                    owner,
                    both[i],
                )
                for i in range(2)
            )

        none = jnp.zeros((tiles, 16, 128), i16)
        found += lax.fori_loop(0, full // 128, search, (none, none), unroll=4)
    owner_columns = [
        jnp.sum(
            one.reshape(line_count, 128).astype(jnp.int32).astype(f32), axis=1, keepdims=True
        )
        for one in found
    ]
    hits = [jnp.where(column == owners_f32, 1.0, 0.0) for column in owner_columns]
    counts = [jnp.zeros((1, 128), f32)]
    for e in range(experts - 1):
        counts.append(counts[e] + jnp.sum(hits[e], axis=0, keepdims=True))
    fill = jnp.zeros((5, 128), f32)
    slots = []
    for e in range(experts):
        pack = jnp.concatenate([counts[e], offsets, owners_f32, fill], axis=0)
        looked = dot_nt(pack.astype(bf16), hits[e].astype(bf16))
        id_row = id_rows[e : e + 1, 0:line_count]
        id_column = id_columns[:, e : e + 1]
        same = owner_columns[e] == looked[2:3]
        if outgoing:
            rank = jnp.sum(jnp.where(same & (id_column < id_row), 1.0, 0.0), axis=0, keepdims=True)
            slots.append(rank + looked[0:1] + looked[1:2])
        else:
            rank = jnp.sum(jnp.where(same & (id_row < id_column), 1.0, 0.0), axis=1, keepdims=True)
            slots.append(rank + jnp.sum(hits[e] * (counts[e] + offsets), axis=1, keepdims=True))
    return slots


def step_kernel(
    row_count,
    col_count,
    lengths_ref,
    hidden_ref,
    queries_ref,
    new_kv_ref,
    prompt_ref,
    suffix_ref,
    w_out_hbm,
    gain_ref,
    router_ref,
    lines_hbm,
    old_lines_ref,
    new_lines_ref,
    routes_ref,
    layer_ref,
    moved_ref,
    part_out,
    part_in,
    joined_out,
    joined_in,
    heads_in,
    token_in,
    wide,
    summed_out,
    summed_in,
    halved_out,
    halved_in,
    act_in,
    down,
    mixed_out,
    mixed_in,
    nearer_out,
    nearer_in,
    move_out,
    move_in,
    take_slots,
    flat_lines,
    w_out_ref,
    lines_ref,
    local_sems,
    send_sems,
    recv_sems,
):
    row = lax.axis_index("row")
    col = lax.axis_index("col")
    seqs = hidden_ref.shape[0]
    experts, _, line_count, width = lines_hbm.shape
    prompt_rows = prompt_ref.shape[2]
    suffix_rows = suffix_ref.shape[2]
    tokens = seqs * row_count
    share = tokens // col_count
    score_scale = HD ** (-0.5)

    w_out_copy = pltpu.make_async_copy(w_out_hbm, w_out_ref, local_sems.at[0])
    lines_copy = pltpu.make_async_copy(lines_hbm, lines_ref, local_sems.at[1])
    lines_copy.start()
    w_out_copy.start()

    barrier = pltpu.get_barrier_semaphore()
    row_far_count, row_near_count = split(row_count)
    col_far_count, col_near_count = split(col_count)
    row_far, row_near = row // row_near_count, row % row_near_count
    col_far, col_near = col // col_near_count, col % col_near_count

    def col_far_peer(k):
        far = lax.rem(col_far + k, col_far_count)
        return far, {"col": far * col_near_count + col_near}

    def col_near_peer(k):
        near = lax.rem(col_near + k, col_near_count)
        return near, {"col": col_far * col_near_count + near}

    def row_far_peer(k):
        far = lax.rem(row_far + k, row_far_count)
        return far, {"row": far * row_near_count + row_near}

    def row_near_peer(k):
        near = lax.rem(row_near + k, row_near_count)
        return near, {"row": row_far * row_near_count + near}

    def row_peer(k):
        far = lax.rem(row_far + k % row_far_count, row_far_count)
        near = lax.rem(row_near + k // row_far_count, row_near_count)
        peer = far * row_near_count + near
        return peer, {"row": peer}

    def greet(peer_of, count):
        def body(k, carry):
            pl.semaphore_signal(barrier, inc=1, device_id=peer_of(k)[1], device_id_type=MESH)
            return carry

        lax.fori_loop(1, count, body, 0)

    greet(col_far_peer, col_far_count)
    greet(col_near_peer, col_near_count)
    greet(row_peer, row_count)
    greeted = col_far_count + col_near_count + row_count - 3

    def send(peer_of, first, last, lane, source, target):
        def body(k, carry):
            peer, device = peer_of(k)
            pltpu.make_async_remote_copy(
                src_ref=source(peer),
                dst_ref=target(k),
                send_sem=send_sems.at[lane],
                recv_sem=recv_sems.at[lane],
                device_id=device,
                device_id_type=MESH,
            ).start()
            return carry

        lax.fori_loop(first, last, body, 0)

    def wait(lane, copies, sems):
        pltpu.make_async_copy(copies, copies, sems.at[lane]).wait()

    rows = 2 * seqs
    keys = prompt_rows + seqs * suffix_rows
    row_seq = lax.broadcasted_iota(jnp.int32, (rows, keys), 0) % seqs
    lane = lax.broadcasted_iota(jnp.int32, (rows, keys), 1)
    own_lane = lane - prompt_rows
    filled = jnp.zeros((rows, keys), jnp.int32)
    for s in range(seqs):
        filled = jnp.where(row_seq == s, lengths_ref[s], filled)
    slot = col * suffix_rows + own_lane % suffix_rows
    live = (lane < prompt_rows) | ((own_lane // suffix_rows == row_seq) & (slot < filled))

    def query_rows(start):
        first = queries_ref[:, pl.ds(start, HD)].astype(f32)
        second = queries_ref[:, pl.ds(start + HD, HD)].astype(f32)
        return jnp.concatenate([first, second], axis=0)

    def cached(which, head):
        lanes = slice(head * HD, (head + 1) * HD)
        suffix = suffix_ref[:, which, :, lanes].astype(f32).reshape(seqs * suffix_rows, HD)
        return jnp.concatenate([prompt_ref[0, which, :, lanes], suffix.astype(bf16)], axis=0)

    scores = []
    for head in range(col_count):
        scores.append(
            dot_nt(query_rows(2 * head * HD).astype(bf16), cached(0, head)) * score_scale
        )
    half = lax.broadcasted_iota(jnp.int32, (rows, HD), 1) < HD // 2
    for head in range(col_count):
        score = jnp.where(live, scores[head], neg_big)
        top = jnp.max(score, axis=1, keepdims=True).astype(bf16).astype(f32)
        weights = jnp.where(live, jnp.exp(score - top), 0.0)
        total = jnp.sum(weights, axis=1, keepdims=True)
        mixture = jnp.dot(weights.astype(bf16), cached(1, head), preferred_element_type=f32)
        near, far = head % col_near_count, head // col_near_count
        part_out[near, far, 0:rows, :] = mixture.astype(bf16)
        part_out[near, far, rows : 2 * rows, :] = jnp.where(half, top, total).astype(bf16)

    pl.semaphore_wait(barrier, greeted)
    near_parts = part_in.at[pl.ds(1, col_near_count - 1)]
    send(
        col_near_peer,
        1,
        col_near_count,
        0,
        lambda peer: part_out.at[peer],
        lambda k: part_in.at[k],
    )

    per_peer = experts * line_count // row_count
    block = move_out.shape[1]
    slots = line_slots(row, row_count, block, old_lines_ref, new_lines_ref, line_count, True)
    padded = 256
    spare_lanes = jnp.full((1, padded - line_count), -1.0, f32)
    send_slots = jnp.concatenate(
        [part for e in range(experts) for part in (slots[e], spare_lanes)], axis=1
    ).astype(jnp.int32)
    send_slots = jnp.broadcast_to(send_slots, (16, experts * padded)).astype(i16)[None]
    peers_at_once = row_count // 2
    chunk = peers_at_once * block
    lines_copy.wait()
    for e in range(experts):
        at = e * padded
        for j in range(3):
            flat_lines[at : at + line_count, j * width : (j + 1) * width] = lines_ref[e, j]
        flat_lines[at + line_count : at + padded, :] = jnp.zeros(
            (padded - line_count, 3 * width), bf16
        )
    one, zero = jnp.ones((), bf16), jnp.zeros((), bf16)

    def sort_lines(at):
        shape = (chunk // 16, 16, experts * padded)
        place = (
            lax.broadcasted_iota(jnp.int32, (chunk, 128), 0) + at * chunk
        ).astype(i16).reshape(chunk // 16, 16, 128)
        picks = jnp.concatenate(
            [
                jnp.where(place == send_slots[:, :, k * 128 : (k + 1) * 128], one, zero)
                for k in range(experts * padded // 128)
            ],
            axis=2,
        ).reshape(chunk, experts * padded)
        sorted_lines = jnp.dot(picks, flat_lines[...], preferred_element_type=f32).astype(bf16)
        move_out[pl.ds(at * peers_at_once, peers_at_once)] = sorted_lines.reshape(
            peers_at_once, block, 3 * width
        )

    moves = [1 + (row_count - 1) * share_of // 31 for share_of in MOVES]

    early = row_count // 2

    def move(batch):
        send(
            row_peer,
            moves[batch],
            moves[batch + 1],
            12 if moves[batch + 1] <= early else 13,
            lambda peer: move_out.at[peer],
            lambda k: move_in.at[k],
        )

    def join(parts, tops):
        top = tops[0]
        for other in tops[1:]:
            top = jnp.maximum(top, other)
        total = jnp.zeros((rows, HD), f32)
        mixture = jnp.zeros((rows, HD), f32)
        for part in parts:
            stats = part[rows : 2 * rows].astype(f32)
            factor = jnp.exp(stats[:, 0:1] - top)
            total = total + factor * stats
            mixture = mixture + factor * part[0:rows].astype(f32)
        return top, total[:, HD // 2 : HD // 2 + 1], mixture

    def top_of(part):
        return part[rows : 2 * rows].astype(f32)[:, 0:1]

    part_in[0] = part_out[col_near]
    wait(0, near_parts, recv_sems)
    for far in range(col_far_count):
        parts = [part_in[k, far] for k in range(col_near_count)]
        top, total, mixture = join(parts, [top_of(part) for part in parts])
        joined_out[far, 0:rows, :] = mixture.astype(bf16)
        joined_out[far, rows : 2 * rows, :] = jnp.where(half, top, total).astype(bf16)
    far_parts = joined_in.at[pl.ds(1, col_far_count - 1)]
    send(
        col_far_peer,
        1,
        col_far_count,
        1,
        lambda peer: joined_out.at[peer],
        lambda k: joined_in.at[k],
    )
    sort_lines(0)
    sort_lines(1)
    move_in[0] = move_out[row]
    move(0)

    joined_in[0] = joined_out[col_far]
    own_query = query_rows(pl.multiple_of(col * 2 * HD, 2 * HD))
    own_pair = new_kv_ref[:, :, pl.ds(pl.multiple_of(col * HD, HD), HD)].astype(f32)
    own_key = jnp.concatenate([own_pair[:, 0, :]] * 2, axis=0)
    own_value = jnp.concatenate([own_pair[:, 1, :]] * 2, axis=0)
    own_score = jnp.sum(own_query * own_key, axis=1, keepdims=True) * score_scale
    wait(1, far_parts, recv_sems)
    parts = [joined_in[k] for k in range(col_far_count)]
    top, total, mixture = join(parts, [top_of(part) for part in parts] + [own_score])
    own_weight = jnp.exp(own_score - top)
    mixture = mixture + own_weight.astype(bf16).astype(f32) * own_value
    heads_in[0, col_far] = (mixture / (total + own_weight)).astype(bf16)
    own_heads = heads_in.at[0, col_far]
    far_heads = heads_in.at[0, pl.ds(0, col_far_count - 1)]
    near_heads = heads_in.at[pl.ds(1, col_near_count - 1)]
    send(col_far_peer, 1, col_far_count, 2, lambda peer: own_heads, lambda k: own_heads)
    move(1)

    tail = line_count - 128
    for e in range(experts):
        lanes = slice(e * width, (e + 1) * width)
        wide[0:128, lanes] = lines_ref[e, 0, 0:128, :]
        wide[128:256, lanes] = lines_ref[e, 1, 0:128, :]
        wide[256 : 256 + tail, lanes] = lines_ref[e, 0, 128:line_count, :]
        wide[256 + tail : 256 + 2 * tail, lanes] = lines_ref[e, 1, 128:line_count, :]
        spare = 128 - 2 * tail
        router_row = jnp.broadcast_to(router_ref[e : e + 1, :].astype(f32), (spare, width))
        first = lax.broadcasted_iota(jnp.int32, (spare, width), 0) == 0
        wide[256 + 2 * tail : 384, lanes] = jnp.where(first, router_row, 0.0).astype(bf16)
        gap = jnp.zeros((64 - tail, width), bf16)
        down[e, 0:line_count, :] = lines_ref[e, 2]
        down[e, line_count : 128 + 64, :] = gap
        down[e, 192 : 192 + tail, :] = lines_ref[e, 2, 128:line_count, :]
        down[e, 192 + tail : 256, :] = gap

    wait(2, far_heads, recv_sems)
    send(
        col_near_peer,
        1,
        col_near_count,
        3,
        lambda peer: heads_in.at[0],
        lambda k: heads_in.at[k],
    )
    move(2)
    wait(3, near_heads, recv_sems)
    w_out_copy.wait()
    projected = jnp.zeros((rows, 2 * width), f32)
    for k in range(col_near_count):
        near = lax.rem(col_near + col_near_count - k, col_near_count)
        for far in range(col_far_count):
            head = far * col_near_count + near
            start = pl.multiple_of(head * 2 * HD, 2 * HD)
            pair = jnp.concatenate(
                [w_out_ref[pl.ds(start, HD), :], w_out_ref[pl.ds(start + HD, HD), :]], axis=1
            )
            projected = projected + jnp.dot(heads_in[k, far], pair, preferred_element_type=f32)
    projected = projected[0:seqs, 0:width] + projected[seqs:rows, width : 2 * width]
    h_float = (hidden_ref[...].astype(f32) + projected).astype(bf16).astype(f32)
    scaled = h_float * gain_ref[...].astype(f32)
    squares = jnp.sum(h_float * h_float, axis=1, keepdims=True)
    high = squares.astype(bf16).astype(f32)
    half = lax.broadcasted_iota(jnp.int32, (seqs, width), 1) < width // 2
    message = jnp.concatenate([scaled, jnp.where(half, high, squares - high)], axis=0).astype(bf16)
    token_in[row_near, row_far] = message
    own_tokens = token_in.at[row_near, row_far]
    far_tokens = token_in.at[0, pl.ds(0, row_far_count - 1)]
    near_tokens = token_in.at[pl.ds(0, row_near_count - 1)]
    send(row_far_peer, 1, row_far_count, 4, lambda peer: own_tokens, lambda k: own_tokens)
    move(3)

    for e, slots in enumerate(
        line_slots(row, row_count, block, new_lines_ref, old_lines_ref, line_count, False)
    ):
        take_slots[e] = jnp.broadcast_to(slots, (line_count, 128)).astype(jnp.int32).astype(i16)
    routes = [
        jnp.transpose(jnp.broadcast_to(routes_ref[k : k + 1, :].astype(f32), (width, tokens)))
        for k in range(2)
    ]

    wait(4, far_tokens, recv_sems)
    own_tokens = token_in.at[row_near]
    send(row_near_peer, 1, row_near_count, 5, lambda peer: own_tokens, lambda k: own_tokens)
    move(4)
    wait(5, near_tokens, recv_sems)
    everything = token_in[...].astype(f32)
    by_row = [everything[r % row_near_count, r // row_near_count] for r in range(row_count)]
    every_token = jnp.concatenate([part[0:seqs] for part in by_row], axis=0)
    every_square = jnp.concatenate([part[seqs : 2 * seqs] for part in by_row], axis=0)
    square = every_square[:, 0:1] + every_square[:, width // 2 : width // 2 + 1]
    token_lane = lax.broadcasted_iota(jnp.int32, (tokens, 128), 1)
    at = 2 * tail

    def with_spares(last, logit, square):
        spare = lax.broadcasted_iota(jnp.int32, last.shape, len(last.shape) - 1) - at
        logit_high = logit.astype(bf16).astype(f32)
        square_high = square.astype(bf16).astype(f32)
        last = jnp.where(spare == 0, logit_high, last)
        last = jnp.where(spare == 1, logit - logit_high, last)
        last = jnp.where(spare == 2, square_high, last)
        return jnp.where(spare == 3, square - square_high, last)

    for k in range(2):
        masked = jnp.concatenate(
            [jnp.where(routes[k] == e, every_token, 0.0).astype(bf16) for e in range(experts)],
            axis=1,
        )
        picked = dot_nt(masked, wide[...])
        last = picked[:, 256:384]
        last = with_spares(last, last[:, at : at + 1], square)
        picked = jnp.concatenate([picked[:, 0:256], last], axis=1).astype(bf16)
        for c in range(col_count):
            summed_out[c % col_near_count, c // col_near_count, k] = picked[
                c * share : (c + 1) * share
            ]
    near_sums = summed_in.at[pl.ds(1, col_near_count - 1)]
    far_sums = halved_in.at[pl.ds(1, col_far_count - 1)]
    send(
        col_near_peer,
        1,
        col_near_count,
        6,
        lambda peer: summed_out.at[peer],
        lambda k: summed_in.at[k],
    )
    move(5)

    summed_in[0] = summed_out[col_near]
    wait(6, near_sums, recv_sems)
    for far in range(col_far_count):
        sums = summed_in[0, far].astype(f32)
        for k in range(1, col_near_count):
            sums = sums + summed_in[k, far].astype(f32)
        last = sums[:, :, 256:384]
        logit = last[:, :, at : at + 1] + last[:, :, at + 1 : at + 2]
        square = last[:, :, at + 2 : at + 3] + last[:, :, at + 3 : at + 4]
        halved_out[far, :, :, 0:256] = sums[:, :, 0:256].astype(bf16)
        halved_out[far, :, :, 256:384] = with_spares(last, logit, square).astype(bf16)
    send(
        col_far_peer,
        1,
        col_far_count,
        7,
        lambda peer: halved_out.at[peer],
        lambda k: halved_in.at[k],
    )
    move(6)
    halved_in[0] = halved_out[col_far]
    wait(7, far_sums, recv_sems)
    sums = halved_in[0].astype(f32)
    for k in range(1, col_far_count):
        sums = sums + halved_in[k].astype(f32)
    last = sums[:, :, 256:384]
    square = last[:, :, at + 2 : at + 3] + last[:, :, at + 3 : at + 4]
    inverse_rms = lax.rsqrt(square / (width * col_count) + norm_eps)
    logits = (last[:, :, at : at + 1] + last[:, :, at + 1 : at + 2]) * inverse_rms
    logits = jnp.exp(logits - jnp.max(logits, axis=0, keepdims=True))
    gates = logits / jnp.sum(logits, axis=0, keepdims=True)
    last = last.reshape(2 * share, 128)
    shifted = pltpu.roll(last, 128 - tail, 1).reshape(2, share, 128)
    last = last.reshape(2, share, 128)

    def activated(gate, up):
        gate = gate * inverse_rms
        return gate / (1.0 + jnp.exp(-gate)) * (up * inverse_rms) * gates

    act_first = activated(sums[:, :, 0:128], sums[:, :, 128:256])
    act_last = activated(last, shifted)
    share_lane = lax.broadcasted_iota(jnp.int32, (share, 128), 1)
    second = pltpu.roll(act_last[1], 64, 1)
    ends = jnp.where(
        share_lane < tail,
        act_last[0],
        jnp.where((share_lane >= 64) & (share_lane < 64 + tail), second, 0.0),
    )
    message = jnp.concatenate([act_first[0], act_first[1], ends], axis=0).astype(bf16)
    act_in[col_near, col_far] = message.reshape(3, share, 128)
    own_acts = act_in.at[col_near, col_far]
    far_acts = act_in.at[0, pl.ds(0, col_far_count - 1)]
    near_acts = act_in.at[pl.ds(0, col_near_count - 1)]
    send(col_far_peer, 1, col_far_count, 8, lambda peer: own_acts, lambda k: own_acts)
    move(7)
    wait(8, far_acts, recv_sems)
    own_row = act_in.at[col_near]
    send(col_near_peer, 1, col_near_count, 9, lambda peer: own_row, lambda k: own_row)
    move(8)

    wait(9, near_acts, recv_sems)
    by_col = [act_in[c % col_near_count, c // col_near_count] for c in range(col_count)]
    firsts = [
        jnp.concatenate([part[k] for part in by_col], axis=0).astype(f32) for k in range(2)
    ]
    ends = jnp.concatenate([part[2] for part in by_col], axis=0).astype(f32)
    end_route = jnp.where(token_lane < 64, routes[0], routes[1])
    mixed = jnp.zeros((tokens, width), f32)
    for e in range(experts):
        begin = jnp.where(routes[0] == e, firsts[0], jnp.where(routes[1] == e, firsts[1], 0.0))
        end = jnp.where(end_route == e, ends, 0.0)
        both = jnp.concatenate([begin, end], axis=1).astype(bf16)
        mixed = mixed + jnp.dot(both, down[e], preferred_element_type=f32)
    for r in range(row_count):
        mixed_out[r % row_near_count, r // row_near_count] = mixed[
            r * seqs : (r + 1) * seqs
        ].astype(bf16)
    near_mixed = mixed_in.at[pl.ds(1, row_near_count - 1)]
    far_mixed = nearer_in.at[pl.ds(1, row_far_count - 1)]
    send(
        row_near_peer,
        1,
        row_near_count,
        10,
        lambda peer: mixed_out.at[peer],
        lambda k: mixed_in.at[k],
    )
    move(9)
    mixed_in[0] = mixed_out[row_near]
    wait(10, near_mixed, recv_sems)
    nearer_out[...] = jnp.sum(mixed_in[...].astype(f32), axis=0).astype(bf16)
    send(
        row_far_peer,
        1,
        row_far_count,
        11,
        lambda peer: nearer_out.at[peer],
        lambda k: nearer_in.at[k],
    )
    move(10)
    nearer_in[0] = nearer_out[row_far]

    early_moved = move_in.at[pl.ds(1, early - 1)]
    late_moved = move_in.at[pl.ds(early, row_count - early)]

    def place_lines(start, add):
        here = move_in[pl.ds(start, early)].reshape(early * block, 3 * width)
        place = lax.broadcasted_iota(jnp.int32, (16, 128), 1) + start * block
        at_once = experts // 2
        for e in range(0, experts, at_once):
            taken = take_slots[e : e + at_once].reshape(at_once * line_count // 16, 16, 128)
            picks = jnp.concatenate(
                [
                    jnp.where(taken == (place + k * 128).astype(i16)[None], one, zero)
                    for k in range(early * block // 128)
                ],
                axis=2,
            ).reshape(at_once * line_count, early * block)
            placed = jnp.dot(picks, here, preferred_element_type=f32).astype(bf16)
            for i in range(at_once):
                for j in range(3):
                    part = placed[i * line_count : (i + 1) * line_count, j * width : (j + 1) * width]
                    moved_ref[e + i, j] = moved_ref[e + i, j] + part if add else part

    wait(12, early_moved, recv_sems)
    place_lines(0, False)
    wait(11, far_mixed, recv_sems)
    layer_ref[...] = h_float + jnp.sum(nearer_in[...].astype(f32), axis=0)

    wait(13, late_moved, recv_sems)
    place_lines(early, True)

    sent = [near_parts, far_parts, far_heads, near_heads, far_tokens, near_tokens, near_sums]
    sent += [far_sums, far_acts, near_acts, near_mixed, far_mixed, early_moved]
    sent += [late_moved]
    for lane, copies in enumerate(sent):
        wait(lane, copies, send_sems)


def local(
    row_count,
    col_count,
    hidden,
    queries,
    new_kv,
    prompt_kv,
    suffix_kv,
    lengths,
    w_out,
    moe_gain,
    w_router,
    expert_weights,
    old_lines,
    new_lines,
    routes,
):
    experts, line_count, parts, width = expert_weights.shape
    seqs = hidden.shape[0]
    tokens = seqs * row_count
    share = tokens // col_count
    per_peer = experts * line_count // row_count
    block = rounded_up(per_peer, 16)
    row_far, row_near = split(row_count)
    col_far, col_near = split(col_count)
    vmem = pl.BlockSpec(memory_space=pltpu.VMEM)
    hbm = pl.BlockSpec(memory_space=pl.ANY)
    rows = 2 * seqs
    layer_out, moved = pl.pallas_call(
        functools.partial(step_kernel, row_count, col_count),
        out_shape=(
            jax.ShapeDtypeStruct((seqs, width), f32),
            jax.ShapeDtypeStruct((experts, parts, line_count, width), bf16),
        ),
        in_specs=[pl.BlockSpec(memory_space=pltpu.SMEM)] + [vmem] * 5 + [hbm, vmem, vmem, hbm] + [vmem] * 3,
        out_specs=(vmem, vmem),
        scratch_shapes=[
            pltpu.VMEM((col_near, col_far, 2 * rows, HD), bf16),
            pltpu.VMEM((col_near, col_far, 2 * rows, HD), bf16),
            pltpu.VMEM((col_far, 2 * rows, HD), bf16),
            pltpu.VMEM((col_far, 2 * rows, HD), bf16),
            pltpu.VMEM((col_near, col_far, rows, HD), bf16),
            pltpu.VMEM((row_near, row_far, rows, width), bf16),
            pltpu.VMEM((384, experts * width), bf16),
            pltpu.VMEM((col_near, col_far, 2, share, 384), bf16),
            pltpu.VMEM((col_near, col_far, 2, share, 384), bf16),
            pltpu.VMEM((col_far, 2, share, 384), bf16),
            pltpu.VMEM((col_far, 2, share, 384), bf16),
            pltpu.VMEM((col_near, col_far, 3, share, 128), bf16),
            pltpu.VMEM((experts, 256, width), bf16),
            pltpu.VMEM((row_near, row_far, seqs, width), bf16),
            pltpu.VMEM((row_near, row_far, seqs, width), bf16),
            pltpu.VMEM((row_far, seqs, width), bf16),
            pltpu.VMEM((row_far, seqs, width), bf16),
            pltpu.VMEM((row_count, block, parts * width), bf16),
            pltpu.VMEM((row_count, block, parts * width), bf16),
            pltpu.VMEM((experts, line_count, 128), i16),
            pltpu.VMEM((experts * 256, parts * width), bf16),
            pltpu.VMEM(w_out.shape, bf16),
            pltpu.VMEM((experts, parts, line_count, width), bf16),
            pltpu.SemaphoreType.DMA((2,)),
            pltpu.SemaphoreType.DMA((14,)),
            pltpu.SemaphoreType.DMA((14,)),
        ],
        compiler_params=pltpu.CompilerParams(
            collective_id=0, has_side_effects=True, vmem_limit_bytes=56 << 20
        ),
        name="decode_step",
    )(
        lengths,
        hidden,
        queries,
        new_kv,
        prompt_kv,
        suffix_kv,
        w_out,
        moe_gain.reshape(1, width),
        jnp.transpose(w_router),
        jnp.transpose(expert_weights, (0, 2, 1, 3)),
        old_lines,
        new_lines,
        jnp.transpose(routes),
    )
    return layer_out, jnp.transpose(moved, (0, 2, 1, 3))


def solution(mesh):
    return jax.shard_map(
        functools.partial(local, mesh.shape["row"], mesh.shape["col"]),
        mesh=mesh,
        in_specs=(
            P("row", "col"),
            P("row", None),
            P("row", None, None),
            P("row", None, "col", None),
            P("row", None, "col", None),
            P("row"),
            P(None, "col"),
            P("col"),
            P("col", None),
            P(None, "row", None, "col"),
            P(),
            P(),
            P(),
        ),
        out_specs=(P("row", "col"), P(None, "row", None, "col")),
        check_vma=False,
    )
```

```python
import functools

import jax
import jax.numpy as jnp
from jax import lax
from jax.experimental import pallas as pl
from jax.experimental.pallas import tpu as pltpu
from jax.sharding import PartitionSpec as P

HD = 128
norm_eps = 1e-06
neg_big = -1e30
f32 = jnp.float32
bf16 = jnp.bfloat16
i16 = jnp.int16
MESH = pl.DeviceIdType.MESH
MOVES = (0, 3, 6, 9, 12, 15, 18, 21, 24, 28, 31)


def rounded_up(value, step):
    return (value + step - 1) // step * step


def dot_nt(a, b):
    return lax.dot_general(a, b, (((1,), (1,)), ((), ())), preferred_element_type=f32)


def split(count):
    far = 4 if count >= 16 else 2
    return far, count // far


def line_slots(row, row_count, block, ids_ref, table_ref, line_count, outgoing):
    experts, full = table_ref.shape
    window = min(full, 512)
    start = row * line_count
    base = jnp.minimum(start // 128 * 128, full - window)
    held = ids_ref[:, pl.ds(pl.multiple_of(base, 128), window)]
    held = pltpu.roll(held, lax.rem(window - (start - base), window), 1)[:, 0:256]
    id_rows = held.astype(f32)
    padded = jnp.concatenate([id_rows, jnp.zeros((128 - experts, 256), f32)], axis=0)
    id_columns = jnp.transpose(padded)[0:line_count]
    owner_lane = lax.broadcasted_iota(jnp.int32, (1, 128), 1)
    owners_f32 = owner_lane.astype(f32)
    if outgoing:
        offsets = owners_f32 * block
    else:
        far_count, near_count = split(row_count)
        far = lax.rem(row // near_count - owner_lane // near_count + 128 * far_count, far_count)
        near = lax.rem(row % near_count - owner_lane % near_count + near_count, near_count)
        offsets = (near * far_count + far).astype(f32) * block
    tiles = line_count // 16
    wanted = [
        jnp.broadcast_to(id_columns[:, e : e + 1], (line_count, 128))
        .astype(jnp.int32)
        .astype(i16)
        .reshape(tiles, 16, 128)
        for e in range(experts)
    ]

    def rows16(row):
        return jnp.broadcast_to(row, (16, 128)).astype(i16)[None]

    found = []
    for e in range(0, experts, 2):

        def search(chunk, both):
            at = chunk * 128
            first = at // line_count
            owner = rows16(first + jnp.where(owner_lane + at >= (first + 1) * line_count, 1, 0))
            return tuple(
                jnp.where(
                    wanted[e + i]
                    == rows16(
                        table_ref[e + i : e + i + 1, pl.ds(pl.multiple_of(at, 128), 128)]
                    ),
                    owner,
                    both[i],
                )
                for i in range(2)
            )

        none = jnp.zeros((tiles, 16, 128), i16)
        found += lax.fori_loop(0, full // 128, search, (none, none), unroll=4)
    owner_columns = [
        jnp.sum(
            one.reshape(line_count, 128).astype(jnp.int32).astype(f32), axis=1, keepdims=True
        )
        for one in found
    ]
    hits = [jnp.where(column == owners_f32, 1.0, 0.0) for column in owner_columns]
    counts = [jnp.zeros((1, 128), f32)]
    for e in range(experts - 1):
        counts.append(counts[e] + jnp.sum(hits[e], axis=0, keepdims=True))
    fill = jnp.zeros((5, 128), f32)
    slots = []
    for e in range(experts):
        pack = jnp.concatenate([counts[e], offsets, owners_f32, fill], axis=0)
        looked = dot_nt(pack.astype(bf16), hits[e].astype(bf16))
        id_row = id_rows[e : e + 1, 0:line_count]
        id_column = id_columns[:, e : e + 1]
        same = owner_columns[e] == looked[2:3]
        if outgoing:
            rank = jnp.sum(jnp.where(same & (id_column < id_row), 1.0, 0.0), axis=0, keepdims=True)
            slots.append(rank + looked[0:1] + looked[1:2])
        else:
            rank = jnp.sum(jnp.where(same & (id_row < id_column), 1.0, 0.0), axis=1, keepdims=True)
            slots.append(rank + jnp.sum(hits[e] * (counts[e] + offsets), axis=1, keepdims=True))
    return slots


def step_kernel(
    row_count,
    col_count,
    lengths_ref,
    hidden_ref,
    queries_ref,
    new_kv_ref,
    prompt_ref,
    suffix_ref,
    w_out_hbm,
    gain_ref,
    router_ref,
    lines_hbm,
    old_lines_ref,
    new_lines_ref,
    routes_ref,
    layer_ref,
    moved_ref,
    part_out,
    part_in,
    joined_out,
    joined_in,
    heads_in,
    token_in,
    wide,
    summed_out,
    summed_in,
    halved_out,
    halved_in,
    act_in,
    down,
    mixed_out,
    mixed_in,
    nearer_out,
    nearer_in,
    move_out,
    move_in,
    take_slots,
    flat_lines,
    w_out_ref,
    lines_ref,
    local_sems,
    send_sems,
    recv_sems,
):
    row = lax.axis_index("row")
    col = lax.axis_index("col")
    seqs = hidden_ref.shape[0]
    experts, _, line_count, width = lines_hbm.shape
    prompt_rows = prompt_ref.shape[2]
    suffix_rows = suffix_ref.shape[2]
    tokens = seqs * row_count
    share = tokens // col_count
    score_scale = HD ** (-0.5)

    w_out_copy = pltpu.make_async_copy(w_out_hbm, w_out_ref, local_sems.at[0])
    lines_copy = pltpu.make_async_copy(lines_hbm, lines_ref, local_sems.at[1])
    lines_copy.start()
    w_out_copy.start()

    barrier = pltpu.get_barrier_semaphore()
    row_far_count, row_near_count = split(row_count)
    col_far_count, col_near_count = split(col_count)
    row_far, row_near = row // row_near_count, row % row_near_count
    col_far, col_near = col // col_near_count, col % col_near_count

    def col_far_peer(k):
        far = lax.rem(col_far + k, col_far_count)
        return far, {"col": far * col_near_count + col_near}

    def col_near_peer(k):
        near = lax.rem(col_near + k, col_near_count)
        return near, {"col": col_far * col_near_count + near}

    def row_far_peer(k):
        far = lax.rem(row_far + k, row_far_count)
        return far, {"row": far * row_near_count + row_near}

    def row_near_peer(k):
        near = lax.rem(row_near + k, row_near_count)
        return near, {"row": row_far * row_near_count + near}

    def row_peer(k):
        far = lax.rem(row_far + k % row_far_count, row_far_count)
        near = lax.rem(row_near + k // row_far_count, row_near_count)
        peer = far * row_near_count + near
        return peer, {"row": peer}

    def greet(peer_of, count):
        def body(k, carry):
            pl.semaphore_signal(barrier, inc=1, device_id=peer_of(k)[1], device_id_type=MESH)
            return carry

        lax.fori_loop(1, count, body, 0)

    greet(col_far_peer, col_far_count)
    greet(col_near_peer, col_near_count)
    greet(row_peer, row_count)
    greeted = col_far_count + col_near_count + row_count - 3

    def send(peer_of, first, last, lane, source, target):
        def body(k, carry):
            peer, device = peer_of(k)
            pltpu.make_async_remote_copy(
                src_ref=source(peer),
                dst_ref=target(k),
                send_sem=send_sems.at[lane],
                recv_sem=recv_sems.at[lane],
                device_id=device,
                device_id_type=MESH,
            ).start()
            return carry

        lax.fori_loop(first, last, body, 0)

    def wait(lane, copies, sems):
        pltpu.make_async_copy(copies, copies, sems.at[lane]).wait()

    rows = 2 * seqs
    keys = prompt_rows + seqs * suffix_rows
    row_seq = lax.broadcasted_iota(jnp.int32, (rows, keys), 0) % seqs
    lane = lax.broadcasted_iota(jnp.int32, (rows, keys), 1)
    own_lane = lane - prompt_rows
    filled = jnp.zeros((rows, keys), jnp.int32)
    for s in range(seqs):
        filled = jnp.where(row_seq == s, lengths_ref[s], filled)
    slot = col * suffix_rows + own_lane % suffix_rows
    live = (lane < prompt_rows) | ((own_lane // suffix_rows == row_seq) & (slot < filled))

    def query_rows(start):
        first = queries_ref[:, pl.ds(start, HD)].astype(f32)
        second = queries_ref[:, pl.ds(start + HD, HD)].astype(f32)
        return jnp.concatenate([first, second], axis=0)

    def cached(which, head):
        lanes = slice(head * HD, (head + 1) * HD)
        suffix = suffix_ref[:, which, :, lanes].astype(f32).reshape(seqs * suffix_rows, HD)
        return jnp.concatenate([prompt_ref[0, which, :, lanes], suffix.astype(bf16)], axis=0)

    scores = []
    for head in range(col_count):
        scores.append(
            dot_nt(query_rows(2 * head * HD).astype(bf16), cached(0, head)) * score_scale
        )
    half = lax.broadcasted_iota(jnp.int32, (rows, HD), 1) < HD // 2
    for head in range(col_count):
        score = jnp.where(live, scores[head], neg_big)
        top = jnp.max(score, axis=1, keepdims=True).astype(bf16).astype(f32)
        weights = jnp.where(live, jnp.exp(score - top), 0.0)
        total = jnp.sum(weights, axis=1, keepdims=True)
        mixture = jnp.dot(weights.astype(bf16), cached(1, head), preferred_element_type=f32)
        near, far = head % col_near_count, head // col_near_count
        part_out[near, far, 0:rows, :] = mixture.astype(bf16)
        part_out[near, far, rows : 2 * rows, :] = jnp.where(half, top, total).astype(bf16)

    pl.semaphore_wait(barrier, greeted)
    near_parts = part_in.at[pl.ds(1, col_near_count - 1)]
    send(
        col_near_peer,
        1,
        col_near_count,
        0,
        lambda peer: part_out.at[peer],
        lambda k: part_in.at[k],
    )

    per_peer = experts * line_count // row_count
    block = move_out.shape[1]
    slots = line_slots(row, row_count, block, old_lines_ref, new_lines_ref, line_count, True)
    padded = 256
    spare_lanes = jnp.full((1, padded - line_count), -1.0, f32)
    send_slots = jnp.concatenate(
        [part for e in range(experts) for part in (slots[e], spare_lanes)], axis=1
    ).astype(jnp.int32)
    send_slots = jnp.broadcast_to(send_slots, (16, experts * padded)).astype(i16)[None]
    peers_at_once = row_count // 2
    chunk = peers_at_once * block
    lines_copy.wait()
    for e in range(experts):
        at = e * padded
        for j in range(3):
            flat_lines[at : at + line_count, j * width : (j + 1) * width] = lines_ref[e, j]
        flat_lines[at + line_count : at + padded, :] = jnp.zeros(
            (padded - line_count, 3 * width), bf16
        )
    one, zero = jnp.ones((), bf16), jnp.zeros((), bf16)

    def sort_lines(at):
        shape = (chunk // 16, 16, experts * padded)
        place = (
            lax.broadcasted_iota(jnp.int32, (chunk, 128), 0) + at * chunk
        ).astype(i16).reshape(chunk // 16, 16, 128)
        picks = jnp.concatenate(
            [
                jnp.where(place == send_slots[:, :, k * 128 : (k + 1) * 128], one, zero)
                for k in range(experts * padded // 128)
            ],
            axis=2,
        ).reshape(chunk, experts * padded)
        sorted_lines = jnp.dot(picks, flat_lines[...], preferred_element_type=f32).astype(bf16)
        move_out[pl.ds(at * peers_at_once, peers_at_once)] = sorted_lines.reshape(
            peers_at_once, block, 3 * width
        )

    moves = [1 + (row_count - 1) * share_of // 31 for share_of in MOVES]

    early = row_count // 2

    def mirrored(k):
        far = k % row_far_count
        turned = lax.rem(row_far_count - far, row_far_count)
        return k - far + jnp.where(row_near % 2 == 1, turned, far)

    def move_peer(k):
        return row_peer(mirrored(k))

    def move(batch):
        send(
            move_peer,
            moves[batch],
            moves[batch + 1],
            11 if moves[batch + 1] <= early else 12,
            lambda peer: move_out.at[peer],
            lambda k: move_in.at[mirrored(k)],
        )

    def join(parts, tops):
        top = tops[0]
        for other in tops[1:]:
            top = jnp.maximum(top, other)
        total = jnp.zeros((rows, HD), f32)
        mixture = jnp.zeros((rows, HD), f32)
        for part in parts:
            stats = part[rows : 2 * rows].astype(f32)
            factor = jnp.exp(stats[:, 0:1] - top)
            total = total + factor * stats
            mixture = mixture + factor * part[0:rows].astype(f32)
        return top, total[:, HD // 2 : HD // 2 + 1], mixture

    def top_of(part):
        return part[rows : 2 * rows].astype(f32)[:, 0:1]

    part_in[0] = part_out[col_near]
    wait(0, near_parts, recv_sems)
    for far in range(col_far_count):
        parts = [part_in[k, far] for k in range(col_near_count)]
        top, total, mixture = join(parts, [top_of(part) for part in parts])
        joined_out[far, 0:rows, :] = mixture.astype(bf16)
        joined_out[far, rows : 2 * rows, :] = jnp.where(half, top, total).astype(bf16)
    far_parts = joined_in.at[pl.ds(1, col_far_count - 1)]
    send(
        col_far_peer,
        1,
        col_far_count,
        1,
        lambda peer: joined_out,
        lambda k: joined_in.at[k],
    )
    sort_lines(0)
    sort_lines(1)
    move_in[0] = move_out[row]
    move(0)

    joined_in[0] = joined_out[...]
    own_pairs = []
    for far in range(col_far_count):
        head = far * col_near_count + col_near
        own_query = query_rows(pl.multiple_of(head * 2 * HD, 2 * HD))
        own_pair = new_kv_ref[:, :, pl.ds(pl.multiple_of(head * HD, HD), HD)].astype(f32)
        own_key = jnp.concatenate([own_pair[:, 0, :]] * 2, axis=0)
        own_value = jnp.concatenate([own_pair[:, 1, :]] * 2, axis=0)
        own_score = jnp.sum(own_query * own_key, axis=1, keepdims=True) * score_scale
        own_pairs.append((own_score, own_value))
    wait(1, far_parts, recv_sems)
    for far in range(col_far_count):
        own_score, own_value = own_pairs[far]
        parts = [joined_in[k, far] for k in range(col_far_count)]
        top, total, mixture = join(parts, [top_of(part) for part in parts] + [own_score])
        own_weight = jnp.exp(own_score - top)
        mixture = mixture + own_weight.astype(bf16).astype(f32) * own_value
        heads_in[0, far] = (mixture / (total + own_weight)).astype(bf16)
    near_heads = heads_in.at[pl.ds(1, col_near_count - 1)]
    send(
        col_near_peer,
        1,
        col_near_count,
        2,
        lambda peer: heads_in.at[0],
        lambda k: heads_in.at[k],
    )
    move(1)

    tail = line_count - 128
    for e in range(experts):
        lanes = slice(e * width, (e + 1) * width)
        wide[0:128, lanes] = lines_ref[e, 0, 0:128, :]
        wide[128:256, lanes] = lines_ref[e, 1, 0:128, :]
        wide[256 : 256 + tail, lanes] = lines_ref[e, 0, 128:line_count, :]
        wide[256 + tail : 256 + 2 * tail, lanes] = lines_ref[e, 1, 128:line_count, :]
        spare = 128 - 2 * tail
        router_row = jnp.broadcast_to(router_ref[e : e + 1, :].astype(f32), (spare, width))
        first = lax.broadcasted_iota(jnp.int32, (spare, width), 0) == 0
        wide[256 + 2 * tail : 384, lanes] = jnp.where(first, router_row, 0.0).astype(bf16)
        gap = jnp.zeros((64 - tail, width), bf16)
        down[e, 0:line_count, :] = lines_ref[e, 2]
        down[e, line_count : 128 + 64, :] = gap
        down[e, 192 : 192 + tail, :] = lines_ref[e, 2, 128:line_count, :]
        down[e, 192 + tail : 256, :] = gap

    wait(2, near_heads, recv_sems)
    w_out_copy.wait()
    projected = jnp.zeros((rows, 2 * width), f32)
    for k in range(col_near_count):
        near = lax.rem(col_near + col_near_count - k, col_near_count)
        for far in range(col_far_count):
            head = far * col_near_count + near
            start = pl.multiple_of(head * 2 * HD, 2 * HD)
            pair = jnp.concatenate(
                [w_out_ref[pl.ds(start, HD), :], w_out_ref[pl.ds(start + HD, HD), :]], axis=1
            )
            projected = projected + jnp.dot(heads_in[k, far], pair, preferred_element_type=f32)
    projected = projected[0:seqs, 0:width] + projected[seqs:rows, width : 2 * width]
    h_float = (hidden_ref[...].astype(f32) + projected).astype(bf16).astype(f32)
    scaled = h_float * gain_ref[...].astype(f32)
    squares = jnp.sum(h_float * h_float, axis=1, keepdims=True)
    high = squares.astype(bf16).astype(f32)
    half = lax.broadcasted_iota(jnp.int32, (seqs, width), 1) < width // 2
    message = jnp.concatenate([scaled, jnp.where(half, high, squares - high)], axis=0).astype(bf16)
    token_in[row_near, row_far] = message
    own_tokens = token_in.at[row_near, row_far]
    far_tokens = token_in.at[0, pl.ds(0, row_far_count - 1)]
    near_tokens = token_in.at[pl.ds(0, row_near_count - 1)]
    send(row_far_peer, 1, row_far_count, 3, lambda peer: own_tokens, lambda k: own_tokens)
    move(2)

    for e, slots in enumerate(
        line_slots(row, row_count, block, new_lines_ref, old_lines_ref, line_count, False)
    ):
        take_slots[e] = jnp.broadcast_to(slots, (line_count, 128)).astype(jnp.int32).astype(i16)
    routes = [
        jnp.transpose(jnp.broadcast_to(routes_ref[k : k + 1, :].astype(f32), (width, tokens)))
        for k in range(2)
    ]

    wait(3, far_tokens, recv_sems)
    own_tokens = token_in.at[row_near]
    send(row_near_peer, 1, row_near_count, 4, lambda peer: own_tokens, lambda k: own_tokens)
    move(3)
    wait(4, near_tokens, recv_sems)
    everything = token_in[...].astype(f32)
    by_row = [everything[r % row_near_count, r // row_near_count] for r in range(row_count)]
    every_token = jnp.concatenate([part[0:seqs] for part in by_row], axis=0)
    every_square = jnp.concatenate([part[seqs : 2 * seqs] for part in by_row], axis=0)
    square = every_square[:, 0:1] + every_square[:, width // 2 : width // 2 + 1]
    token_lane = lax.broadcasted_iota(jnp.int32, (tokens, 128), 1)
    at = 2 * tail

    def with_spares(last, logit, square):
        spare = lax.broadcasted_iota(jnp.int32, last.shape, len(last.shape) - 1) - at
        logit_high = logit.astype(bf16).astype(f32)
        square_high = square.astype(bf16).astype(f32)
        last = jnp.where(spare == 0, logit_high, last)
        last = jnp.where(spare == 1, logit - logit_high, last)
        last = jnp.where(spare == 2, square_high, last)
        return jnp.where(spare == 3, square - square_high, last)

    for k in range(2):
        masked = jnp.concatenate(
            [jnp.where(routes[k] == e, every_token, 0.0).astype(bf16) for e in range(experts)],
            axis=1,
        )
        picked = dot_nt(masked, wide[...])
        last = picked[:, 256:384]
        last = with_spares(last, last[:, at : at + 1], square)
        picked = jnp.concatenate([picked[:, 0:256], last], axis=1).astype(bf16)
        for c in range(col_count):
            summed_out[c % col_near_count, c // col_near_count, k] = picked[
                c * share : (c + 1) * share
            ]
    near_sums = summed_in.at[pl.ds(1, col_near_count - 1)]
    far_sums = halved_in.at[pl.ds(1, col_far_count - 1)]
    send(
        col_near_peer,
        1,
        col_near_count,
        5,
        lambda peer: summed_out.at[peer],
        lambda k: summed_in.at[k],
    )
    move(4)

    summed_in[0] = summed_out[col_near]
    wait(5, near_sums, recv_sems)
    for far in range(col_far_count):
        sums = summed_in[0, far].astype(f32)
        for k in range(1, col_near_count):
            sums = sums + summed_in[k, far].astype(f32)
        last = sums[:, :, 256:384]
        logit = last[:, :, at : at + 1] + last[:, :, at + 1 : at + 2]
        square = last[:, :, at + 2 : at + 3] + last[:, :, at + 3 : at + 4]
        halved_out[far, :, :, 0:256] = sums[:, :, 0:256].astype(bf16)
        halved_out[far, :, :, 256:384] = with_spares(last, logit, square).astype(bf16)
    send(
        col_far_peer,
        1,
        col_far_count,
        6,
        lambda peer: halved_out.at[peer],
        lambda k: halved_in.at[k],
    )
    move(5)
    halved_in[0] = halved_out[col_far]
    wait(6, far_sums, recv_sems)
    sums = halved_in[0].astype(f32)
    for k in range(1, col_far_count):
        sums = sums + halved_in[k].astype(f32)
    last = sums[:, :, 256:384]
    square = last[:, :, at + 2 : at + 3] + last[:, :, at + 3 : at + 4]
    inverse_rms = lax.rsqrt(square / (width * col_count) + norm_eps)
    logits = (last[:, :, at : at + 1] + last[:, :, at + 1 : at + 2]) * inverse_rms
    logits = jnp.exp(logits - jnp.max(logits, axis=0, keepdims=True))
    gates = logits / jnp.sum(logits, axis=0, keepdims=True)
    last = last.reshape(2 * share, 128)
    shifted = pltpu.roll(last, 128 - tail, 1).reshape(2, share, 128)
    last = last.reshape(2, share, 128)

    def activated(gate, up):
        gate = gate * inverse_rms
        return gate / (1.0 + jnp.exp(-gate)) * (up * inverse_rms) * gates

    act_first = activated(sums[:, :, 0:128], sums[:, :, 128:256])
    act_last = activated(last, shifted)
    share_lane = lax.broadcasted_iota(jnp.int32, (share, 128), 1)
    second = pltpu.roll(act_last[1], 64, 1)
    ends = jnp.where(
        share_lane < tail,
        act_last[0],
        jnp.where((share_lane >= 64) & (share_lane < 64 + tail), second, 0.0),
    )
    message = jnp.concatenate([act_first[0], act_first[1], ends], axis=0).astype(bf16)
    act_in[col_near, col_far] = message.reshape(3, share, 128)
    own_acts = act_in.at[col_near, col_far]
    far_acts = act_in.at[0, pl.ds(0, col_far_count - 1)]
    near_acts = act_in.at[pl.ds(0, col_near_count - 1)]
    send(col_far_peer, 1, col_far_count, 7, lambda peer: own_acts, lambda k: own_acts)
    move(6)
    wait(7, far_acts, recv_sems)
    own_row = act_in.at[col_near]
    send(col_near_peer, 1, col_near_count, 8, lambda peer: own_row, lambda k: own_row)
    move(7)

    wait(8, near_acts, recv_sems)
    by_col = [act_in[c % col_near_count, c // col_near_count] for c in range(col_count)]
    firsts = [
        jnp.concatenate([part[k] for part in by_col], axis=0).astype(f32) for k in range(2)
    ]
    ends = jnp.concatenate([part[2] for part in by_col], axis=0).astype(f32)
    end_route = jnp.where(token_lane < 64, routes[0], routes[1])
    mixed = jnp.zeros((tokens, width), f32)
    for e in range(experts):
        begin = jnp.where(routes[0] == e, firsts[0], jnp.where(routes[1] == e, firsts[1], 0.0))
        end = jnp.where(end_route == e, ends, 0.0)
        both = jnp.concatenate([begin, end], axis=1).astype(bf16)
        mixed = mixed + jnp.dot(both, down[e], preferred_element_type=f32)
    for r in range(row_count):
        mixed_out[r % row_near_count, r // row_near_count] = mixed[
            r * seqs : (r + 1) * seqs
        ].astype(bf16)
    near_mixed = mixed_in.at[pl.ds(1, row_near_count - 1)]
    far_mixed = nearer_in.at[pl.ds(1, row_far_count - 1)]
    send(
        row_near_peer,
        1,
        row_near_count,
        9,
        lambda peer: mixed_out.at[peer],
        lambda k: mixed_in.at[k],
    )
    move(8)
    mixed_in[0] = mixed_out[row_near]
    wait(9, near_mixed, recv_sems)
    nearer_out[...] = jnp.sum(mixed_in[...].astype(f32), axis=0).astype(bf16)
    send(
        row_far_peer,
        1,
        row_far_count,
        10,
        lambda peer: nearer_out.at[peer],
        lambda k: nearer_in.at[k],
    )
    move(9)
    nearer_in[0] = nearer_out[row_far]

    early_moved = move_in.at[pl.ds(1, early - 1)]
    late_moved = move_in.at[pl.ds(early, row_count - early)]

    def place_lines(start, add):
        here = move_in[pl.ds(start, early)].reshape(early * block, 3 * width)
        place = lax.broadcasted_iota(jnp.int32, (16, 128), 1) + start * block
        at_once = experts // 2
        for e in range(0, experts, at_once):
            taken = take_slots[e : e + at_once].reshape(at_once * line_count // 16, 16, 128)
            picks = jnp.concatenate(
                [
                    jnp.where(taken == (place + k * 128).astype(i16)[None], one, zero)
                    for k in range(early * block // 128)
                ],
                axis=2,
            ).reshape(at_once * line_count, early * block)
            placed = jnp.dot(picks, here, preferred_element_type=f32).astype(bf16)
            for i in range(at_once):
                for j in range(3):
                    part = placed[i * line_count : (i + 1) * line_count, j * width : (j + 1) * width]
                    moved_ref[e + i, j] = moved_ref[e + i, j] + part if add else part

    wait(11, early_moved, recv_sems)
    place_lines(0, False)
    wait(10, far_mixed, recv_sems)
    layer_ref[...] = h_float + jnp.sum(nearer_in[...].astype(f32), axis=0)

    wait(12, late_moved, recv_sems)
    place_lines(early, True)

    sent = [near_parts, far_parts, near_heads, far_tokens, near_tokens, near_sums]
    sent += [far_sums, far_acts, near_acts, near_mixed, far_mixed, early_moved]
    sent += [late_moved]
    for lane, copies in enumerate(sent):
        wait(lane, copies, send_sems)


def local(
    row_count,
    col_count,
    hidden,
    queries,
    new_kv,
    prompt_kv,
    suffix_kv,
    lengths,
    w_out,
    moe_gain,
    w_router,
    expert_weights,
    old_lines,
    new_lines,
    routes,
):
    experts, line_count, parts, width = expert_weights.shape
    seqs = hidden.shape[0]
    tokens = seqs * row_count
    share = tokens // col_count
    per_peer = experts * line_count // row_count
    block = rounded_up(per_peer, 16)
    row_far, row_near = split(row_count)
    col_far, col_near = split(col_count)
    vmem = pl.BlockSpec(memory_space=pltpu.VMEM)
    hbm = pl.BlockSpec(memory_space=pl.ANY)
    rows = 2 * seqs
    layer_out, moved = pl.pallas_call(
        functools.partial(step_kernel, row_count, col_count),
        out_shape=(
            jax.ShapeDtypeStruct((seqs, width), f32),
            jax.ShapeDtypeStruct((experts, parts, line_count, width), bf16),
        ),
        in_specs=[pl.BlockSpec(memory_space=pltpu.SMEM)] + [vmem] * 5 + [hbm, vmem, vmem, hbm] + [vmem] * 3,
        out_specs=(vmem, vmem),
        scratch_shapes=[
            pltpu.VMEM((col_near, col_far, 2 * rows, HD), bf16),
            pltpu.VMEM((col_near, col_far, 2 * rows, HD), bf16),
            pltpu.VMEM((col_far, 2 * rows, HD), bf16),
            pltpu.VMEM((col_far, col_far, 2 * rows, HD), bf16),
            pltpu.VMEM((col_near, col_far, rows, HD), bf16),
            pltpu.VMEM((row_near, row_far, rows, width), bf16),
            pltpu.VMEM((384, experts * width), bf16),
            pltpu.VMEM((col_near, col_far, 2, share, 384), bf16),
            pltpu.VMEM((col_near, col_far, 2, share, 384), bf16),
            pltpu.VMEM((col_far, 2, share, 384), bf16),
            pltpu.VMEM((col_far, 2, share, 384), bf16),
            pltpu.VMEM((col_near, col_far, 3, share, 128), bf16),
            pltpu.VMEM((experts, 256, width), bf16),
            pltpu.VMEM((row_near, row_far, seqs, width), bf16),
            pltpu.VMEM((row_near, row_far, seqs, width), bf16),
            pltpu.VMEM((row_far, seqs, width), bf16),
            pltpu.VMEM((row_far, seqs, width), bf16),
            pltpu.VMEM((row_count, block, parts * width), bf16),
            pltpu.VMEM((row_count, block, parts * width), bf16),
            pltpu.VMEM((experts, line_count, 128), i16),
            pltpu.VMEM((experts * 256, parts * width), bf16),
            pltpu.VMEM(w_out.shape, bf16),
            pltpu.VMEM((experts, parts, line_count, width), bf16),
            pltpu.SemaphoreType.DMA((2,)),
            pltpu.SemaphoreType.DMA((13,)),
            pltpu.SemaphoreType.DMA((13,)),
        ],
        compiler_params=pltpu.CompilerParams(
            collective_id=0, has_side_effects=True, vmem_limit_bytes=56 << 20
        ),
        name="decode_step",
    )(
        lengths,
        hidden,
        queries,
        new_kv,
        prompt_kv,
        suffix_kv,
        w_out,
        moe_gain.reshape(1, width),
        jnp.transpose(w_router),
        jnp.transpose(expert_weights, (0, 2, 1, 3)),
        old_lines,
        new_lines,
        jnp.transpose(routes),
    )
    return layer_out, jnp.transpose(moved, (0, 2, 1, 3))


def solution(mesh):
    return jax.shard_map(
        functools.partial(local, mesh.shape["row"], mesh.shape["col"]),
        mesh=mesh,
        in_specs=(
            P("row", "col"),
            P("row", None),
            P("row", None, None),
            P("row", None, "col", None),
            P("row", None, "col", None),
            P("row"),
            P(None, "col"),
            P("col"),
            P("col", None),
            P(None, "row", None, "col"),
            P(),
            P(),
            P(),
        ),
        out_specs=(P("row", "col"), P(None, "row", None, "col")),
        check_vma=False,
    )
```

```python
import functools

import jax
import jax.numpy as jnp
from jax import lax
from jax.experimental import pallas as pl
from jax.experimental.pallas import tpu as pltpu
from jax.sharding import PartitionSpec as P

HD = 128
norm_eps = 1e-06
neg_big = -1e30
f32 = jnp.float32
bf16 = jnp.bfloat16
i16 = jnp.int16
MESH = pl.DeviceIdType.MESH
MOVES = (0, 4, 6, 10, 12, 15, 19, 22, 25, 27, 31)


def rounded_up(value, step):
    return (value + step - 1) // step * step


def dot_nt(a, b):
    return lax.dot_general(a, b, (((1,), (1,)), ((), ())), preferred_element_type=f32)


def split(count):
    far = 4 if count >= 16 else 2
    return far, count // far


def line_slots(row, row_count, block, ids_ref, table_ref, line_count, outgoing):
    experts, full = table_ref.shape
    window = min(full, 512)
    start = row * line_count
    base = jnp.minimum(start // 128 * 128, full - window)
    held = ids_ref[:, pl.ds(pl.multiple_of(base, 128), window)]
    held = pltpu.roll(held, lax.rem(window - (start - base), window), 1)[:, 0:256]
    id_rows = held.astype(f32)
    padded = jnp.concatenate([id_rows, jnp.zeros((128 - experts, 256), f32)], axis=0)
    id_columns = jnp.transpose(padded)[0:line_count]
    owner_lane = lax.broadcasted_iota(jnp.int32, (1, 128), 1)
    owners_f32 = owner_lane.astype(f32)
    if outgoing:
        offsets = owners_f32 * block
    else:
        far_count, near_count = split(row_count)
        far = lax.rem(row // near_count - owner_lane // near_count + 128 * far_count, far_count)
        near = lax.rem(row % near_count - owner_lane % near_count + near_count, near_count)
        offsets = (near * far_count + far).astype(f32) * block
    tiles = line_count // 16
    wanted = [
        jnp.broadcast_to(id_columns[:, e : e + 1], (line_count, 128))
        .astype(jnp.int32)
        .astype(i16)
        .reshape(tiles, 16, 128)
        for e in range(experts)
    ]

    def rows16(row):
        return jnp.broadcast_to(row, (16, 128)).astype(i16)[None]

    found = []
    for e in range(0, experts, 2):

        def search(chunk, both):
            at = chunk * 128
            first = at // line_count
            owner = rows16(first + jnp.where(owner_lane + at >= (first + 1) * line_count, 1, 0))
            return tuple(
                jnp.where(
                    wanted[e + i]
                    == rows16(
                        table_ref[e + i : e + i + 1, pl.ds(pl.multiple_of(at, 128), 128)]
                    ),
                    owner,
                    both[i],
                )
                for i in range(2)
            )

        none = jnp.zeros((tiles, 16, 128), i16)
        found += lax.fori_loop(0, full // 128, search, (none, none), unroll=4)
    owner_columns = [
        jnp.sum(
            one.reshape(line_count, 128).astype(jnp.int32).astype(f32), axis=1, keepdims=True
        )
        for one in found
    ]
    hits = [jnp.where(column == owners_f32, 1.0, 0.0) for column in owner_columns]
    counts = [jnp.zeros((1, 128), f32)]
    for e in range(experts - 1):
        counts.append(counts[e] + jnp.sum(hits[e], axis=0, keepdims=True))
    fill = jnp.zeros((5, 128), f32)
    slots = []
    for e in range(experts):
        pack = jnp.concatenate([counts[e], offsets, owners_f32, fill], axis=0)
        looked = dot_nt(pack.astype(bf16), hits[e].astype(bf16))
        id_row = id_rows[e : e + 1, 0:line_count]
        id_column = id_columns[:, e : e + 1]
        same = owner_columns[e] == looked[2:3]
        if outgoing:
            rank = jnp.sum(jnp.where(same & (id_column < id_row), 1.0, 0.0), axis=0, keepdims=True)
            slots.append(rank + looked[0:1] + looked[1:2])
        else:
            rank = jnp.sum(jnp.where(same & (id_row < id_column), 1.0, 0.0), axis=1, keepdims=True)
            slots.append(rank + jnp.sum(hits[e] * (counts[e] + offsets), axis=1, keepdims=True))
    return slots


def step_kernel(
    row_count,
    col_count,
    lengths_ref,
    hidden_ref,
    queries_ref,
    new_kv_ref,
    prompt_ref,
    suffix_ref,
    w_out_hbm,
    gain_ref,
    router_ref,
    lines_hbm,
    old_lines_ref,
    new_lines_ref,
    routes_ref,
    layer_ref,
    moved_ref,
    part_out,
    part_in,
    joined_out,
    joined_in,
    heads_in,
    token_in,
    wide,
    summed_out,
    summed_in,
    halved_out,
    halved_in,
    act_in,
    down,
    mixed_out,
    mixed_in,
    nearer_out,
    nearer_in,
    move_out,
    move_in,
    take_slots,
    flat_lines,
    w_out_ref,
    lines_ref,
    local_sems,
    send_sems,
    recv_sems,
):
    row = lax.axis_index("row")
    col = lax.axis_index("col")
    seqs = hidden_ref.shape[0]
    experts, _, line_count, width = lines_hbm.shape
    prompt_rows = prompt_ref.shape[2]
    suffix_rows = suffix_ref.shape[2]
    tokens = seqs * row_count
    share = tokens // col_count
    score_scale = HD ** (-0.5)

    w_out_copy = pltpu.make_async_copy(w_out_hbm, w_out_ref, local_sems.at[0])
    lines_copy = pltpu.make_async_copy(lines_hbm, lines_ref, local_sems.at[1])
    lines_copy.start()
    w_out_copy.start()

    barrier = pltpu.get_barrier_semaphore()
    row_far_count, row_near_count = split(row_count)
    col_far_count, col_near_count = split(col_count)
    row_far, row_near = row // row_near_count, row % row_near_count
    col_far, col_near = col // col_near_count, col % col_near_count

    def col_far_peer(k):
        far = lax.rem(col_far + k, col_far_count)
        return far, {"col": far * col_near_count + col_near}

    def col_near_peer(k):
        near = lax.rem(col_near + k, col_near_count)
        return near, {"col": col_far * col_near_count + near}

    def row_far_peer(k):
        far = lax.rem(row_far + k, row_far_count)
        return far, {"row": far * row_near_count + row_near}

    def row_near_peer(k):
        near = lax.rem(row_near + k, row_near_count)
        return near, {"row": row_far * row_near_count + near}

    def row_peer(k):
        far = lax.rem(row_far + k % row_far_count, row_far_count)
        near = lax.rem(row_near + k // row_far_count, row_near_count)
        peer = far * row_near_count + near
        return peer, {"row": peer}

    def greet(peer_of, count):
        def body(k, carry):
            pl.semaphore_signal(barrier, inc=1, device_id=peer_of(k)[1], device_id_type=MESH)
            return carry

        lax.fori_loop(1, count, body, 0)

    greet(col_far_peer, col_far_count)
    greet(col_near_peer, col_near_count)
    greet(row_peer, row_count)
    greeted = col_far_count + col_near_count + row_count - 3

    def send(peer_of, first, last, lane, source, target):
        def body(k, carry):
            peer, device = peer_of(k)
            pltpu.make_async_remote_copy(
                src_ref=source(peer),
                dst_ref=target(k),
                send_sem=send_sems.at[lane],
                recv_sem=recv_sems.at[lane],
                device_id=device,
                device_id_type=MESH,
            ).start()
            return carry

        lax.fori_loop(first, last, body, 0)

    def wait(lane, copies, sems):
        pltpu.make_async_copy(copies, copies, sems.at[lane]).wait()

    rows = 2 * seqs
    keys = prompt_rows + seqs * suffix_rows
    row_seq = lax.broadcasted_iota(jnp.int32, (rows, keys), 0) % seqs
    lane = lax.broadcasted_iota(jnp.int32, (rows, keys), 1)
    own_lane = lane - prompt_rows
    filled = jnp.zeros((rows, keys), jnp.int32)
    for s in range(seqs):
        filled = jnp.where(row_seq == s, lengths_ref[s], filled)
    slot = col * suffix_rows + own_lane % suffix_rows
    live = (lane < prompt_rows) | ((own_lane // suffix_rows == row_seq) & (slot < filled))

    def query_rows(start):
        first = queries_ref[:, pl.ds(start, HD)].astype(f32)
        second = queries_ref[:, pl.ds(start + HD, HD)].astype(f32)
        return jnp.concatenate([first, second], axis=0)

    def cached(which, head):
        lanes = slice(head * HD, (head + 1) * HD)
        suffix = suffix_ref[:, which, :, lanes].astype(f32).reshape(seqs * suffix_rows, HD)
        return jnp.concatenate([prompt_ref[0, which, :, lanes], suffix.astype(bf16)], axis=0)

    scores = []
    for head in range(col_count):
        scores.append(
            dot_nt(query_rows(2 * head * HD).astype(bf16), cached(0, head)) * score_scale
        )
    half = lax.broadcasted_iota(jnp.int32, (rows, HD), 1) < HD // 2
    for head in range(col_count):
        score = jnp.where(live, scores[head], neg_big)
        top = jnp.max(score, axis=1, keepdims=True).astype(bf16).astype(f32)
        weights = jnp.where(live, jnp.exp(score - top), 0.0)
        total = jnp.sum(weights, axis=1, keepdims=True)
        mixture = jnp.dot(weights.astype(bf16), cached(1, head), preferred_element_type=f32)
        near, far = head % col_near_count, head // col_near_count
        part_out[near, far, 0:rows, :] = mixture.astype(bf16)
        part_out[near, far, rows : 2 * rows, :] = jnp.where(half, top, total).astype(bf16)

    pl.semaphore_wait(barrier, greeted)
    near_parts = part_in.at[pl.ds(1, col_near_count - 1)]
    send(
        col_near_peer,
        1,
        col_near_count,
        0,
        lambda peer: part_out.at[peer],
        lambda k: part_in.at[k],
    )

    per_peer = experts * line_count // row_count
    block = move_out.shape[1]
    slots = line_slots(row, row_count, block, old_lines_ref, new_lines_ref, line_count, True)
    padded = 256
    spare_lanes = jnp.full((1, padded - line_count), -1.0, f32)
    send_slots = jnp.concatenate(
        [part for e in range(experts) for part in (slots[e], spare_lanes)], axis=1
    ).astype(jnp.int32)
    send_slots = jnp.broadcast_to(send_slots, (16, experts * padded)).astype(i16)[None]
    peers_at_once = row_count // 2
    chunk = peers_at_once * block
    lines_copy.wait()
    for e in range(experts):
        at = e * padded
        for j in range(3):
            flat_lines[at : at + line_count, j * width : (j + 1) * width] = lines_ref[e, j]
        flat_lines[at + line_count : at + padded, :] = jnp.zeros(
            (padded - line_count, 3 * width), bf16
        )
    one, zero = jnp.ones((), bf16), jnp.zeros((), bf16)

    def sort_lines(at):
        shape = (chunk // 16, 16, experts * padded)
        place = (
            lax.broadcasted_iota(jnp.int32, (chunk, 128), 0) + at * chunk
        ).astype(i16).reshape(chunk // 16, 16, 128)
        picks = jnp.concatenate(
            [
                jnp.where(place == send_slots[:, :, k * 128 : (k + 1) * 128], one, zero)
                for k in range(experts * padded // 128)
            ],
            axis=2,
        ).reshape(chunk, experts * padded)
        sorted_lines = jnp.dot(picks, flat_lines[...], preferred_element_type=f32).astype(bf16)
        move_out[pl.ds(at * peers_at_once, peers_at_once)] = sorted_lines.reshape(
            peers_at_once, block, 3 * width
        )

    moves = [1 + (row_count - 1) * share_of // 31 for share_of in MOVES]

    early = row_count // 2

    def mirrored(k):
        far = k % row_far_count
        turned = lax.rem(row_far_count - far, row_far_count)
        return k - far + jnp.where(row_near % 2 == 1, turned, far)

    def move_peer(k):
        return row_peer(mirrored(k))

    def move(batch):
        send(
            move_peer,
            moves[batch],
            moves[batch + 1],
            11 if moves[batch + 1] <= early else 12,
            lambda peer: move_out.at[peer],
            lambda k: move_in.at[mirrored(k)],
        )

    def join(parts, tops):
        top = tops[0]
        for other in tops[1:]:
            top = jnp.maximum(top, other)
        total = jnp.zeros((rows, HD), f32)
        mixture = jnp.zeros((rows, HD), f32)
        for part in parts:
            stats = part[rows : 2 * rows].astype(f32)
            factor = jnp.exp(stats[:, 0:1] - top)
            total = total + factor * stats
            mixture = mixture + factor * part[0:rows].astype(f32)
        return top, total[:, HD // 2 : HD // 2 + 1], mixture

    def top_of(part):
        return part[rows : 2 * rows].astype(f32)[:, 0:1]

    part_in[0] = part_out[col_near]
    wait(0, near_parts, recv_sems)
    for far in range(col_far_count):
        parts = [part_in[k, far] for k in range(col_near_count)]
        top, total, mixture = join(parts, [top_of(part) for part in parts])
        joined_out[far, 0:rows, :] = mixture.astype(bf16)
        joined_out[far, rows : 2 * rows, :] = jnp.where(half, top, total).astype(bf16)
    far_parts = joined_in.at[pl.ds(1, col_far_count - 1)]
    send(
        col_far_peer,
        1,
        col_far_count,
        1,
        lambda peer: joined_out,
        lambda k: joined_in.at[k],
    )
    sort_lines(0)
    sort_lines(1)
    move_in[0] = move_out[row]
    move(0)

    joined_in[0] = joined_out[...]
    own_pairs = []
    for far in range(col_far_count):
        head = far * col_near_count + col_near
        own_query = query_rows(pl.multiple_of(head * 2 * HD, 2 * HD))
        own_pair = new_kv_ref[:, :, pl.ds(pl.multiple_of(head * HD, HD), HD)].astype(f32)
        own_key = jnp.concatenate([own_pair[:, 0, :]] * 2, axis=0)
        own_value = jnp.concatenate([own_pair[:, 1, :]] * 2, axis=0)
        own_score = jnp.sum(own_query * own_key, axis=1, keepdims=True) * score_scale
        own_pairs.append((own_score, own_value))
    wait(1, far_parts, recv_sems)
    for far in range(col_far_count):
        own_score, own_value = own_pairs[far]
        parts = [joined_in[k, far] for k in range(col_far_count)]
        top, total, mixture = join(parts, [top_of(part) for part in parts] + [own_score])
        own_weight = jnp.exp(own_score - top)
        mixture = mixture + own_weight.astype(bf16).astype(f32) * own_value
        heads_in[0, far] = (mixture / (total + own_weight)).astype(bf16)
    near_heads = heads_in.at[pl.ds(1, col_near_count - 1)]
    send(
        col_near_peer,
        1,
        col_near_count,
        2,
        lambda peer: heads_in.at[0],
        lambda k: heads_in.at[k],
    )
    move(1)

    tail = line_count - 128
    for e in range(experts):
        lanes = slice(e * width, (e + 1) * width)
        wide[0:128, lanes] = lines_ref[e, 0, 0:128, :]
        wide[128:256, lanes] = lines_ref[e, 1, 0:128, :]
        wide[256 : 256 + tail, lanes] = lines_ref[e, 0, 128:line_count, :]
        wide[256 + tail : 256 + 2 * tail, lanes] = lines_ref[e, 1, 128:line_count, :]
        spare = 128 - 2 * tail
        router_row = jnp.broadcast_to(router_ref[e : e + 1, :].astype(f32), (spare, width))
        first = lax.broadcasted_iota(jnp.int32, (spare, width), 0) == 0
        wide[256 + 2 * tail : 384, lanes] = jnp.where(first, router_row, 0.0).astype(bf16)
        gap = jnp.zeros((64 - tail, width), bf16)
        down[e, 0:line_count, :] = lines_ref[e, 2]
        down[e, line_count : 128 + 64, :] = gap
        down[e, 192 : 192 + tail, :] = lines_ref[e, 2, 128:line_count, :]
        down[e, 192 + tail : 256, :] = gap

    wait(2, near_heads, recv_sems)
    w_out_copy.wait()
    projected = jnp.zeros((rows, 2 * width), f32)
    for k in range(col_near_count):
        near = lax.rem(col_near + col_near_count - k, col_near_count)
        for far in range(col_far_count):
            head = far * col_near_count + near
            start = pl.multiple_of(head * 2 * HD, 2 * HD)
            pair = jnp.concatenate(
                [w_out_ref[pl.ds(start, HD), :], w_out_ref[pl.ds(start + HD, HD), :]], axis=1
            )
            projected = projected + jnp.dot(heads_in[k, far], pair, preferred_element_type=f32)
    projected = projected[0:seqs, 0:width] + projected[seqs:rows, width : 2 * width]
    h_float = (hidden_ref[...].astype(f32) + projected).astype(bf16).astype(f32)
    scaled = h_float * gain_ref[...].astype(f32)
    squares = jnp.sum(h_float * h_float, axis=1, keepdims=True)
    high = squares.astype(bf16).astype(f32)
    half = lax.broadcasted_iota(jnp.int32, (seqs, width), 1) < width // 2
    message = jnp.concatenate([scaled, jnp.where(half, high, squares - high)], axis=0).astype(bf16)
    token_in[row_near, row_far] = message
    own_tokens = token_in.at[row_near, row_far]
    far_tokens = token_in.at[0, pl.ds(0, row_far_count - 1)]
    near_tokens = token_in.at[pl.ds(0, row_near_count - 1)]
    send(row_far_peer, 1, row_far_count, 3, lambda peer: own_tokens, lambda k: own_tokens)
    move(2)

    for e, slots in enumerate(
        line_slots(row, row_count, block, new_lines_ref, old_lines_ref, line_count, False)
    ):
        take_slots[e] = jnp.broadcast_to(slots, (line_count, 128)).astype(jnp.int32).astype(i16)
    routes = [
        jnp.transpose(jnp.broadcast_to(routes_ref[k : k + 1, :].astype(f32), (width, tokens)))
        for k in range(2)
    ]

    wait(3, far_tokens, recv_sems)
    own_tokens = token_in.at[row_near]
    send(row_near_peer, 1, row_near_count, 4, lambda peer: own_tokens, lambda k: own_tokens)
    move(3)
    wait(4, near_tokens, recv_sems)
    everything = token_in[...].astype(f32)
    by_row = [everything[r % row_near_count, r // row_near_count] for r in range(row_count)]
    every_token = jnp.concatenate([part[0:seqs] for part in by_row], axis=0)
    every_square = jnp.concatenate([part[seqs : 2 * seqs] for part in by_row], axis=0)
    square = every_square[:, 0:1] + every_square[:, width // 2 : width // 2 + 1]
    token_lane = lax.broadcasted_iota(jnp.int32, (tokens, 128), 1)
    at = 2 * tail

    def with_spares(last, logit, square):
        spare = lax.broadcasted_iota(jnp.int32, last.shape, len(last.shape) - 1) - at
        logit_high = logit.astype(bf16).astype(f32)
        square_high = square.astype(bf16).astype(f32)
        last = jnp.where(spare == 0, logit_high, last)
        last = jnp.where(spare == 1, logit - logit_high, last)
        last = jnp.where(spare == 2, square_high, last)
        return jnp.where(spare == 3, square - square_high, last)

    for k in range(2):
        masked = jnp.concatenate(
            [jnp.where(routes[k] == e, every_token, 0.0).astype(bf16) for e in range(experts)],
            axis=1,
        )
        picked = dot_nt(masked, wide[...])
        last = picked[:, 256:384]
        last = with_spares(last, last[:, at : at + 1], square)
        picked = jnp.concatenate([picked[:, 0:256], last], axis=1).astype(bf16)
        for c in range(col_count):
            summed_out[c % col_near_count, c // col_near_count, k] = picked[
                c * share : (c + 1) * share
            ]
    near_sums = summed_in.at[pl.ds(1, col_near_count - 1)]
    far_sums = halved_in.at[pl.ds(1, col_far_count - 1)]
    send(
        col_near_peer,
        1,
        col_near_count,
        5,
        lambda peer: summed_out.at[peer],
        lambda k: summed_in.at[k],
    )
    move(4)

    summed_in[0] = summed_out[col_near]
    wait(5, near_sums, recv_sems)
    for far in range(col_far_count):
        sums = summed_in[0, far].astype(f32)
        for k in range(1, col_near_count):
            sums = sums + summed_in[k, far].astype(f32)
        last = sums[:, :, 256:384]
        logit = last[:, :, at : at + 1] + last[:, :, at + 1 : at + 2]
        square = last[:, :, at + 2 : at + 3] + last[:, :, at + 3 : at + 4]
        halved_out[far, :, :, 0:256] = sums[:, :, 0:256].astype(bf16)
        halved_out[far, :, :, 256:384] = with_spares(last, logit, square).astype(bf16)
    send(
        col_far_peer,
        1,
        col_far_count,
        6,
        lambda peer: halved_out.at[peer],
        lambda k: halved_in.at[k],
    )
    move(5)
    halved_in[0] = halved_out[col_far]
    wait(6, far_sums, recv_sems)
    sums = halved_in[0].astype(f32)
    for k in range(1, col_far_count):
        sums = sums + halved_in[k].astype(f32)
    last = sums[:, :, 256:384]
    square = last[:, :, at + 2 : at + 3] + last[:, :, at + 3 : at + 4]
    inverse_rms = lax.rsqrt(square / (width * col_count) + norm_eps)
    logits = (last[:, :, at : at + 1] + last[:, :, at + 1 : at + 2]) * inverse_rms
    logits = jnp.exp(logits - jnp.max(logits, axis=0, keepdims=True))
    gates = logits / jnp.sum(logits, axis=0, keepdims=True)
    last = last.reshape(2 * share, 128)
    shifted = pltpu.roll(last, 128 - tail, 1).reshape(2, share, 128)
    last = last.reshape(2, share, 128)

    def activated(gate, up):
        gate = gate * inverse_rms
        return gate / (1.0 + jnp.exp(-gate)) * (up * inverse_rms) * gates

    act_first = activated(sums[:, :, 0:128], sums[:, :, 128:256])
    act_last = activated(last, shifted)
    share_lane = lax.broadcasted_iota(jnp.int32, (share, 128), 1)
    second = pltpu.roll(act_last[1], 64, 1)
    ends = jnp.where(
        share_lane < tail,
        act_last[0],
        jnp.where((share_lane >= 64) & (share_lane < 64 + tail), second, 0.0),
    )
    message = jnp.concatenate([act_first[0], act_first[1], ends], axis=0).astype(bf16)
    act_in[col_near, col_far] = message.reshape(3, share, 128)
    own_acts = act_in.at[col_near, col_far]
    far_acts = act_in.at[0, pl.ds(0, col_far_count - 1)]
    near_acts = act_in.at[pl.ds(0, col_near_count - 1)]
    send(col_far_peer, 1, col_far_count, 7, lambda peer: own_acts, lambda k: own_acts)
    move(6)
    wait(7, far_acts, recv_sems)
    own_row = act_in.at[col_near]
    send(col_near_peer, 1, col_near_count, 8, lambda peer: own_row, lambda k: own_row)
    move(7)

    wait(8, near_acts, recv_sems)
    by_col = [act_in[c % col_near_count, c // col_near_count] for c in range(col_count)]
    firsts = [
        jnp.concatenate([part[k] for part in by_col], axis=0).astype(f32) for k in range(2)
    ]
    ends = jnp.concatenate([part[2] for part in by_col], axis=0).astype(f32)
    end_route = jnp.where(token_lane < 64, routes[0], routes[1])
    mixed = jnp.zeros((tokens, width), f32)
    for e in range(experts):
        begin = jnp.where(routes[0] == e, firsts[0], jnp.where(routes[1] == e, firsts[1], 0.0))
        end = jnp.where(end_route == e, ends, 0.0)
        both = jnp.concatenate([begin, end], axis=1).astype(bf16)
        mixed = mixed + jnp.dot(both, down[e], preferred_element_type=f32)
    for r in range(row_count):
        mixed_out[r % row_near_count, r // row_near_count] = mixed[
            r * seqs : (r + 1) * seqs
        ].astype(bf16)
    near_mixed = mixed_in.at[pl.ds(1, row_near_count - 1)]
    far_mixed = nearer_in.at[pl.ds(1, row_far_count - 1)]
    send(
        row_near_peer,
        1,
        row_near_count,
        9,
        lambda peer: mixed_out.at[peer],
        lambda k: mixed_in.at[k],
    )
    move(8)
    mixed_in[0] = mixed_out[row_near]
    wait(9, near_mixed, recv_sems)
    nearer_out[...] = jnp.sum(mixed_in[...].astype(f32), axis=0).astype(bf16)
    send(
        row_far_peer,
        1,
        row_far_count,
        10,
        lambda peer: nearer_out.at[peer],
        lambda k: nearer_in.at[k],
    )
    move(9)
    nearer_in[0] = nearer_out[row_far]

    early_moved = move_in.at[pl.ds(1, early - 1)]
    late_moved = move_in.at[pl.ds(early, row_count - early)]

    def place_lines(start, add):
        here = move_in[pl.ds(start, early)].reshape(early * block, 3 * width)
        place = lax.broadcasted_iota(jnp.int32, (16, 128), 1) + start * block
        at_once = experts // 2
        for e in range(0, experts, at_once):
            taken = take_slots[e : e + at_once].reshape(at_once * line_count // 16, 16, 128)
            picks = jnp.concatenate(
                [
                    jnp.where(taken == (place + k * 128).astype(i16)[None], one, zero)
                    for k in range(early * block // 128)
                ],
                axis=2,
            ).reshape(at_once * line_count, early * block)
            placed = jnp.dot(picks, here, preferred_element_type=f32).astype(bf16)
            for i in range(at_once):
                for j in range(3):
                    part = placed[i * line_count : (i + 1) * line_count, j * width : (j + 1) * width]
                    moved_ref[e + i, j] = moved_ref[e + i, j] + part if add else part

    wait(11, early_moved, recv_sems)
    place_lines(0, False)
    wait(10, far_mixed, recv_sems)
    layer_ref[...] = h_float + jnp.sum(nearer_in[...].astype(f32), axis=0)

    wait(12, late_moved, recv_sems)
    place_lines(early, True)

    sent = [near_parts, far_parts, near_heads, far_tokens, near_tokens, near_sums]
    sent += [far_sums, far_acts, near_acts, near_mixed, far_mixed, early_moved]
    sent += [late_moved]
    for lane, copies in enumerate(sent):
        wait(lane, copies, send_sems)


def local(
    row_count,
    col_count,
    hidden,
    queries,
    new_kv,
    prompt_kv,
    suffix_kv,
    lengths,
    w_out,
    moe_gain,
    w_router,
    expert_weights,
    old_lines,
    new_lines,
    routes,
):
    experts, line_count, parts, width = expert_weights.shape
    seqs = hidden.shape[0]
    tokens = seqs * row_count
    share = tokens // col_count
    per_peer = experts * line_count // row_count
    block = rounded_up(per_peer, 16)
    row_far, row_near = split(row_count)
    col_far, col_near = split(col_count)
    vmem = pl.BlockSpec(memory_space=pltpu.VMEM)
    hbm = pl.BlockSpec(memory_space=pl.ANY)
    rows = 2 * seqs
    layer_out, moved = pl.pallas_call(
        functools.partial(step_kernel, row_count, col_count),
        out_shape=(
            jax.ShapeDtypeStruct((seqs, width), f32),
            jax.ShapeDtypeStruct((experts, parts, line_count, width), bf16),
        ),
        in_specs=[pl.BlockSpec(memory_space=pltpu.SMEM)] + [vmem] * 5 + [hbm, vmem, vmem, hbm] + [vmem] * 3,
        out_specs=(vmem, vmem),
        scratch_shapes=[
            pltpu.VMEM((col_near, col_far, 2 * rows, HD), bf16),
            pltpu.VMEM((col_near, col_far, 2 * rows, HD), bf16),
            pltpu.VMEM((col_far, 2 * rows, HD), bf16),
            pltpu.VMEM((col_far, col_far, 2 * rows, HD), bf16),
            pltpu.VMEM((col_near, col_far, rows, HD), bf16),
            pltpu.VMEM((row_near, row_far, rows, width), bf16),
            pltpu.VMEM((384, experts * width), bf16),
            pltpu.VMEM((col_near, col_far, 2, share, 384), bf16),
            pltpu.VMEM((col_near, col_far, 2, share, 384), bf16),
            pltpu.VMEM((col_far, 2, share, 384), bf16),
            pltpu.VMEM((col_far, 2, share, 384), bf16),
            pltpu.VMEM((col_near, col_far, 3, share, 128), bf16),
            pltpu.VMEM((experts, 256, width), bf16),
            pltpu.VMEM((row_near, row_far, seqs, width), bf16),
            pltpu.VMEM((row_near, row_far, seqs, width), bf16),
            pltpu.VMEM((row_far, seqs, width), bf16),
            pltpu.VMEM((row_far, seqs, width), bf16),
            pltpu.VMEM((row_count, block, parts * width), bf16),
            pltpu.VMEM((row_count, block, parts * width), bf16),
            pltpu.VMEM((experts, line_count, 128), i16),
            pltpu.VMEM((experts * 256, parts * width), bf16),
            pltpu.VMEM(w_out.shape, bf16),
            pltpu.VMEM((experts, parts, line_count, width), bf16),
            pltpu.SemaphoreType.DMA((2,)),
            pltpu.SemaphoreType.DMA((13,)),
            pltpu.SemaphoreType.DMA((13,)),
        ],
        compiler_params=pltpu.CompilerParams(
            collective_id=0, has_side_effects=True, vmem_limit_bytes=56 << 20
        ),
        name="decode_step",
    )(
        lengths,
        hidden,
        queries,
        new_kv,
        prompt_kv,
        suffix_kv,
        w_out,
        moe_gain.reshape(1, width),
        jnp.transpose(w_router),
        jnp.transpose(expert_weights, (0, 2, 1, 3)),
        old_lines,
        new_lines,
        jnp.transpose(routes),
    )
    return layer_out, jnp.transpose(moved, (0, 2, 1, 3))


def solution(mesh):
    return jax.shard_map(
        functools.partial(local, mesh.shape["row"], mesh.shape["col"]),
        mesh=mesh,
        in_specs=(
            P("row", "col"),
            P("row", None),
            P("row", None, None),
            P("row", None, "col", None),
            P("row", None, "col", None),
            P("row"),
            P(None, "col"),
            P("col"),
            P("col", None),
            P(None, "row", None, "col"),
            P(),
            P(),
            P(),
        ),
        out_specs=(P("row", "col"), P(None, "row", None, "col")),
        check_vma=False,
    )
```
